32 devices in a mesh: seq: 4 (over y, x), tp: 8 (over z, core).
Axes of the slice: x: 2, y: 2, z: 4, core: 2. Of those that a mesh axis runs over, the one named last changes fastest.
Arguments:
- tokens: bfloat16 [2048, 2560], P('seq'), may hold values from -6 to 6
- expert_ids: int32 [2048, 6], P('seq'), may hold values from 0 to 15, all different within a row; in each aligned block of 512 rows (0 to 511, 512 to 1023, ...) at most 288 rows name the same one
- gate_weights: bfloat16 [2048, 6], P('seq'), may hold values from 0.049804688 to 0.34960938
- live: int32 [2048], P('seq'), may hold values 0 or 1
- norm_gain: float32 [2560], replicated, may hold values from 0.5 to 1.5
- expert_gate: bfloat16 [16, 1536, 2560], P('tp', 'seq'), may hold values from -0.125 to 0.125
- expert_up: bfloat16 [16, 1536, 2560], P('tp', 'seq'), may hold values from -0.125 to 0.125
- expert_down: bfloat16 [16, 1536, 2560], P('tp', 'seq'), may hold values from -0.15625 to 0.15625
- shared_gate: bfloat16 [1536, 2560], P('seq'), may hold values from -0.125 to 0.125
- shared_up: bfloat16 [1536, 2560], P('seq'), may hold values from -0.125 to 0.125
- shared_down: bfloat16 [1536, 2560], P('seq'), may hold values from -0.15625 to 0.15625
Outputs:
- mixed: bfloat16 [2048, 2560], P(('seq', 'tp'))
The draws below stay inside these ranges and needn't reach their ends.
Inputs may be any that keep to these rules, and one draw needn't show every extreme that they name: `expert_ids`: each row names 6 different experts. In each aligned block of 512 rows (the tokens of one index of seq) no expert is named by more than 288 rows, a bound that some block reaches.
All inputs are finite; a program needn't handle non-finite values. No bound on the sum of `live` on one device may be relied on, other than what follows from the above.
Results may differ from the reference program's by a relative error of at most 0.017.
Values may be sent and summed in bfloat16 or wider, within the bound.
A program may use at most 128 MiB of HBM per device.

```python
import math
import jax
import jax.numpy as jnp
import numpy as np
from jax import lax

D = 2560
FF = 1536
TOP = 6
SH = 1536
TOK_SEQ = 512
EXPERTS = 16
TOKENS = 2048
CAP = 288
N_SEQ = 4


def place_ends(entries, stream_key, least, top_value):
    longest = entries.shape.index(max(entries.shape))
    spots = []
    for shift in (0, 1):
        where = [jax.random.randint(jax.random.fold_in(stream_key, axis), (), 0, length) for axis, length in enumerate(entries.shape)]
        where[longest] = (where[longest] + shift) % entries.shape[longest]
        spots.append(tuple(where))
    return entries.at[spots[0]].set(least).at[spots[1]].set(top_value)


def block_scale(rng, dims, split, smallest, top_value):
    loudness, own = 1.0, jax.random.fold_in(rng, 6)
    for axis_at, parts in split:
        heights = jnp.exp(jax.random.uniform(jax.random.fold_in(own, axis_at), (parts,), jnp.float32, smallest / len(split), top_value / len(split)))
        loudness = loudness * jnp.repeat(heights, dims[axis_at] // parts).reshape([-1 if axis == axis_at else 1 for axis in range(len(dims))])
    return loudness


def deal_out(own_key, own, number, rows, count, top, reach, skew):
    sequence = jax.random.permutation(own_key, count)
    crowded, ordinary = shares(count, rows * top, reach, skew, True), shares(count, rows * top, reach, skew, False)
    places = jnp.arange(count)

    def named(sizes, turn):
        used = int((sizes > 0).sum())
        fixed = max(1, used // 4)
        moved = fixed + (places - fixed + turn * (used - fixed)) % max(1, count - fixed)
        return jnp.zeros((count,), jnp.int32).at[sequence[jnp.where(places < fixed, places, moved)]].set(jnp.asarray(sizes, jnp.int32))

    sizes = jnp.where(number % 4 == 0, named(crowded, number // 4), named(ordinary, number - number // 4 - 1))
    mixed = jax.random.permutation(jax.random.fold_in(own, 3), count)
    donor, receiver = mixed[0:count // 2 * 2:2], mixed[1:count // 2 * 2:2]
    margin = jnp.minimum(sizes[donor] - 1, reach - sizes[receiver]) // 2
    margin = jnp.where((donor == sequence[0]) | (receiver == sequence[0]) | (sizes[receiver] == 0), 0, jnp.maximum(margin, 0))
    moved = jax.random.randint(jax.random.fold_in(own, 4), (count // 2,), 0, 1 << 20) % (margin + 1)
    sizes = sizes.at[donor].add(-moved).at[receiver].add(moved)
    members = jnp.searchsorted(jnp.cumsum(sizes), jnp.arange(rows * top), side="right").astype(jnp.int32)
    listing = members.reshape(top, rows).T
    listing = listing[jax.random.permutation(jax.random.fold_in(own, 1), rows)]
    turn = jax.random.randint(jax.random.fold_in(own, 2), (rows, 1), 0, top)
    return jnp.take_along_axis(listing, (jnp.arange(top)[None, :] + turn) % top, axis=1)


def shares(count, total, bound, lean, full):
    loads = [(1 << 20) // math.isqrt(standing ** lean) + 1 for standing in range(1, count + 1)]
    largest = bound if full else min(bound, max(-(-total // count), total * loads[0] // sum(loads)))
    least = 1 if total - largest >= count - 1 else 0
    given, rest = [largest] + [least] * (count - 1), total - largest - least * (count - 1)
    while rest > 0:
        free = [i for i in range(1, count) if given[i] < largest] or [i for i in range(1, count) if given[i] < bound]
        mass, remaining = sum([loads[i] for i in free]), rest
        for i in free:
            extra = min(bound - given[i], max(1, remaining * loads[i] // mass), rest)
            given[i] = given[i] + extra
            rest = rest - extra
    return np.array(given)


def bell_draw(stream_key, dims, spread, reach, pieces=(), kind=jnp.bfloat16):
    loudness = block_scale(stream_key, dims, pieces, -0.22, 0.18) if pieces else 1.0
    array = jax.random.normal(stream_key, dims, jnp.float32) * spread * loudness
    return jnp.minimum(jnp.maximum(array, -reach), reach).astype(kind)


def setup_inputs(seed: int = 0) -> dict:
    streams_of = jax.random.split(jax.random.key(seed), 12)
    tokens = bell_draw(streams_of[0], (TOKENS, D), 1.0, 6.0, ((0, 4),))
    expert_ids_keys = jax.random.split(jax.random.fold_in(streams_of[1], 1), TOKENS // TOK_SEQ)
    expert_ids_turns = jax.random.permutation(jax.random.fold_in(streams_of[1], 3), TOKENS // TOK_SEQ)
    expert_ids = jax.vmap(lambda own, number: deal_out(jax.random.fold_in(streams_of[1], 2), own, number, TOK_SEQ, EXPERTS, TOP, CAP, 2))(expert_ids_keys, expert_ids_turns).reshape((TOKENS, TOP))
    gate_weights = jnp.clip(0.049804688 + 0.2998047 * jax.random.uniform(streams_of[2], (TOKENS, TOP), jnp.float32) ** block_scale(streams_of[2], (TOKENS, TOP), ((0, 4),), -0.2, 0.2), 0.049804688, 0.34960938).astype(jnp.bfloat16)
    live = place_ends((jax.random.randint(streams_of[3], (TOKENS,), 0, 8) < 7).astype(jnp.int32), jax.random.fold_in(streams_of[3], 1), 0, 1)
    norm_gain = jnp.clip(1.0 + 0.1 * jax.random.normal(streams_of[4], (D,), jnp.float32), 0.5, 1.5)
    expert_gate = bell_draw(streams_of[5], (EXPERTS, FF, D), D ** -0.5, 0.125, ((0, 8), (1, 4)))
    expert_up = bell_draw(streams_of[6], (EXPERTS, FF, D), D ** -0.5, 0.125, ((0, 8), (1, 4)))
    expert_down = bell_draw(streams_of[7], (EXPERTS, FF, D), FF ** -0.5, 0.15625, ((0, 8), (1, 4)))
    shared_gate = bell_draw(streams_of[8], (SH, D), D ** -0.5, 0.125, ((0, 4),))
    shared_up = bell_draw(streams_of[9], (SH, D), D ** -0.5, 0.125, ((0, 4),))
    shared_down = bell_draw(streams_of[10], (SH, D), SH ** -0.5, 0.15625, ((0, 4),))
    return {"tokens": tokens, "expert_ids": expert_ids, "gate_weights": gate_weights, "live": live, "norm_gain": norm_gain, "expert_gate": expert_gate, "expert_up": expert_up, "expert_down": expert_down, "shared_gate": shared_gate, "shared_up": shared_up, "shared_down": shared_down}


def ffn_blocks(rows, w_gate, w_up, w_down, blocks):
    gate_part = jnp.einsum('rd,hd->rh', rows, w_gate, preferred_element_type=jnp.float32)
    up_part = jnp.einsum('rd,hd->rh', rows, w_up, preferred_element_type=jnp.float32)
    hidden = (jax.nn.silu(gate_part) * up_part).astype(jnp.bfloat16)
    row_count = rows.shape[0]
    inner = w_down.shape[0] // blocks
    split_hidden = hidden.astype(jnp.float32).reshape(row_count, blocks, inner)
    split_down = w_down.astype(jnp.float32).reshape(blocks, inner, w_down.shape[1])
    partial_sums = jnp.einsum('rjh,jhd->rjd', split_hidden, split_down)
    rounded = lax.optimization_barrier(partial_sums.astype(jnp.bfloat16))
    return lax.optimization_barrier(jnp.sum(rounded.astype(jnp.float32), axis=1))

def reference(tokens, expert_ids, gate_weights, live, norm_gain, expert_gate, expert_up, expert_down, shared_gate, shared_up, shared_down):
    values = tokens.astype(jnp.float32)
    scale = lax.rsqrt(lax.optimization_barrier(jnp.mean(values * values, axis=-1, keepdims=True)) + 1e-05)
    normed = (values * scale * norm_gain).astype(jnp.bfloat16)
    weight_eff = gate_weights.astype(jnp.float32) * live.astype(jnp.float32)[:, None]
    ids_blocks = expert_ids.reshape(N_SEQ, TOK_SEQ, TOP)
    weight_blocks = weight_eff.reshape(N_SEQ, TOK_SEQ, TOP)
    block_index = jnp.broadcast_to(jnp.arange(N_SEQ, dtype=jnp.int32)[:, None], (N_SEQ, TOK_SEQ)).astype(jnp.int32)
    token_index = (block_index * TOK_SEQ + jnp.arange(TOK_SEQ, dtype=jnp.int32)[None, :]).astype(jnp.int32)

    def one_expert(routed, inputs):
        w_gate, w_up, w_down, expert_index = inputs
        matches = ids_blocks == expert_index
        matched = jnp.any(matches, axis=-1)
        weight = lax.optimization_barrier(jnp.sum(jnp.where(matches, weight_blocks, jnp.zeros_like(weight_blocks)), axis=-1))
        position = jnp.cumsum(matched.astype(jnp.int32), axis=1).astype(jnp.int32) - 1
        slot_pos = jnp.where(matched, position, CAP).astype(jnp.int32)
        slot_token = jnp.full((N_SEQ, CAP), TOKENS, jnp.int32).at[block_index, slot_pos].set(token_index, mode='drop')
        slot_weight = jnp.zeros((N_SEQ, CAP), jnp.float32).at[block_index, slot_pos].set(weight, mode='drop')
        flat_token = slot_token.reshape(-1).astype(jnp.int32)
        valid = flat_token < TOKENS
        picked = normed[jnp.minimum(flat_token, TOKENS - 1)]
        rows = jnp.where(valid[:, None], picked, jnp.zeros_like(picked))
        expert_out = ffn_blocks(rows, w_gate, w_up, w_down, N_SEQ)
        routed = routed.at[flat_token].add(expert_out * slot_weight.reshape(-1)[:, None], mode='drop')
        return (routed, None)
    routed, unused = lax.scan(one_expert, jnp.zeros((TOKENS, D), jnp.float32), (expert_gate, expert_up, expert_down, jnp.arange(EXPERTS, dtype=jnp.int32)))
    shared_blocks = normed.reshape(N_SEQ, TOK_SEQ, D)
    shared_out = lax.map(lambda rows: ffn_blocks(rows, shared_gate, shared_up, shared_down, N_SEQ), shared_blocks)
    return (routed + shared_out.reshape(TOKENS, D)).astype(jnp.bfloat16)
```

```python
import math
from functools import partial

import jax
import jax.numpy as jnp
from jax import lax
from jax.experimental import pallas as pl
from jax.experimental.pallas import tpu as pltpu
from jax.sharding import PartitionSpec as P

MESH = pl.DeviceIdType.MESH
LANES = 128
OWN, A, B, DIAG = 0, 1, 2, 3


def dot_nt(a, b):
    return lax.dot_general(a, b, (((1,), (1,)), ((), ())), preferred_element_type=jnp.float32)


def silu(v):
    return v / (1.0 + jnp.exp(-v))


def layer_kernel(
    chunks,
    n_z,
    columns,
    width,
    rows_z,
    share,
    tok_hbm,
    gain_ref,
    ids_ref,
    gates_ref,
    live_ref,
    gate_hbm,
    up_hbm,
    down_hbm,
    sgate_hbm,
    sup_hbm,
    sdown_hbm,
    out_ref,
    x_buf,
    part,
    from_sib,
    ring_in,
    z_in,
    gate_w,
    up_w,
    down_w,
    sgate_w,
    sup_w,
    sdown_w,
    hid,
    shid,
    tok_v,
    lists,
    w_buf,
    w_sem,
    own_sem,
    send_list,
    send_own,
    send_fwd,
    send_part,
    send_ring,
    send_z,
    recv_list,
    recv_x,
    recv_part,
    recv_ring,
    recv_z,
):
    seq = lax.axis_index("seq")
    tp = lax.axis_index("tp")
    core = tp % 2
    zed = tp // 2
    other = 1 - core
    sx = seq % 2
    sy = seq // 2
    nbr_x = sy * 2 + (1 - sx)
    nbr_y = (1 - sy) * 2 + sx
    sib = (seq, zed * 2 + other)
    dev_a = (nbr_y * other + nbr_x * core, tp)
    dev_b = (nbr_x * other + nbr_y * core, tp)
    dev_d = (3 - seq, tp)
    rows = n_z * rows_z
    parity = zed % 2
    dev_z = (seq, (zed + 1 - 2 * parity) * 2 + core)
    fetched = pl.ds(pl.multiple_of(parity * share, LANES), width - share)
    passed = pl.ds(pl.multiple_of(parity * (width - share), LANES), share)
    given = pl.ds(pl.multiple_of((1 - parity) * (width - share), LANES), share)
    whole = pl.ds(0, width)
    inner = gate_w.shape[0] // columns
    tok_seq = ids_ref.shape[1]
    pair = min(2, chunks)
    pairs = chunks // pair

    def remote(src, dst, ssem, rsem, dev):
        return pltpu.make_async_remote_copy(
            src_ref=src, dst_ref=dst, send_sem=ssem, recv_sem=rsem, device_id=dev, device_id_type=MESH
        )

    def x_copy(k, src_slot, dst_slot, half, cols, ssem, kind, dev):
        return remote(
            x_buf.at[k, src_slot, half, :, cols],
            x_buf.at[k, dst_slot, half, :, cols],
            ssem,
            recv_x.at[k, dst_slot, kind],
            dev,
        )

    def own_a(k):
        return x_copy(k, OWN, A, core, fetched, send_own.at[k, 1], 0, dev_a)

    def own_b(k):
        return x_copy(k, OWN, B, core, fetched, send_own.at[k, 2], 0, dev_b)

    def own_sib(k, half):
        return x_copy(k, OWN, OWN, half, whole, send_own.at[k, 0], 2, sib)

    def net(k, slot):
        return x_copy(k, slot, slot, core, fetched, send_fwd.at[k, 0], 0, dev_a)

    def relay(k):
        return x_copy(k, B, DIAG, core, fetched, send_fwd.at[k, 0], 0, dev_a)

    def over_z(k, slot):
        return x_copy(k, slot, slot, core, passed, send_fwd.at[k, slot], 1, dev_z)

    def from_z(k, slot):
        return x_copy(k, slot, slot, core, given, send_fwd.at[k, slot], 1, dev_z)

    def sib_net(k, slot, half):
        return x_copy(k, slot, slot, half, fetched, send_fwd.at[k, slot + 3], 2, sib)

    def sib_z(k, slot, half):
        return x_copy(k, slot, slot, half, given, send_fwd.at[k, slot + 6], 3, sib)

    def got_net(k, slot):
        net(k, slot).wait_recv()
        over_z(k, slot).start()
        sib_net(k, slot, core).start()

    def got_z(k, slot):
        from_z(k, slot).wait_recv()
        sib_z(k, slot, core).start()

    def got_sib(k, slot):
        sib_net(k, slot, other).wait_recv()
        sib_z(k, slot, other).wait_recv()

    def list_copy(slot, dev):
        return remote(lists.at[OWN], lists.at[slot], send_list.at[slot - 1], recv_list.at[slot - 1], dev)

    def part_copy(k, slot):
        return remote(
            part.at[k, slot, other],
            from_sib.at[k, slot],
            send_part.at[k, slot],
            recv_part.at[k, slot],
            sib,
        )

    def ring_copy(k, slot, leg, dev):
        return remote(
            part.at[k, slot, core],
            ring_in.at[k, leg],
            send_ring.at[k, leg],
            recv_ring.at[k, leg],
            dev,
        )

    def ring_d(k):
        return ring_copy(k, DIAG, 0, dev_a)

    def ring_a(k):
        return ring_copy(k, A, 1, dev_a)

    def ring_b(k):
        return ring_copy(k, B, 2, dev_b)

    def z_copy(k, src_z, dst_z):
        return remote(
            part.at[k, OWN, core, pl.ds(dst_z * rows_z, rows_z)],
            z_in.at[k, src_z],
            send_z.at[k, dst_z],
            recv_z.at[k, src_z],
            (seq, dst_z * 2 + core),
        )

    weight_copies = [
        pltpu.make_async_copy(src, dst, w_sem.at[i])
        for i, (src, dst) in enumerate(
            (
                (gate_hbm, gate_w),
                (up_hbm, up_w),
                (down_hbm, down_w),
                (sgate_hbm, sgate_w),
                (sup_hbm, sup_w),
                (sdown_hbm, sdown_w),
            )
        )
    ]

    def load_own(k):
        return pltpu.make_async_copy(tok_hbm.at[:, core, k], tok_v.at[k], own_sem.at[k])

    def norm_own(k):
        values = tok_v[k].reshape(rows, width).astype(jnp.float32)
        scale = lax.rsqrt(jnp.mean(values * values, axis=-1, keepdims=True) + 1e-05)
        gain = gain_ref[...].reshape(1, width)
        x_buf[k, OWN, core] = (values * scale * gain).astype(jnp.bfloat16)

    def list_own():
        weight = gates_ref[...].astype(jnp.float32) * live_ref[...].reshape(1, tok_seq).astype(jnp.float32)
        expert = lax.broadcasted_iota(jnp.int32, lists.shape[1:], 0)
        total = jnp.zeros(lists.shape[1:], jnp.float32)
        for j in range(ids_ref.shape[0]):
            total = total + jnp.where(ids_ref[j : j + 1] == expert, weight[j : j + 1], 0.0)
        lists[OWN] = total.astype(jnp.bfloat16)

    def spread_weights():
        token = lax.broadcasted_iota(jnp.int32, (1, tok_seq), 1)
        bits_r = rows_z.bit_length() - 1
        bits_k = chunks.bit_length() - 1
        at_r = token & (rows_z - 1)
        at_k = (token >> bits_r) & (chunks - 1)
        at_half = (token >> (bits_r + bits_k)) & 1
        at_z = token >> (bits_r + bits_k + 1)
        place = (at_half * chunks + at_k) * rows + at_z * rows_z + at_r
        row = lax.broadcasted_iota(jnp.int32, (tok_seq, tok_seq), 0)
        onehot = jnp.where(row == place, 1.0, 0.0).astype(jnp.bfloat16)
        expert = lax.broadcasted_iota(jnp.int32, lists.shape[1:], 0)
        for slot in range(4):
            if slot:
                list_copy(slot, dev_a).wait_recv()
            listed = lists[slot].astype(jnp.float32)
            picked = []
            for i in range(columns):
                mine = jnp.where(expert == tp * columns + i, listed, 0.0)
                mine = jnp.sum(mine, axis=0, keepdims=True)
                picked.append(jnp.broadcast_to(mine, (LANES, tok_seq)))
            spread = dot_nt(onehot, jnp.concatenate(picked, axis=0).astype(jnp.bfloat16))
            swapped = {OWN: OWN, A: B, B: A, DIAG: DIAG}[slot]
            for half in range(2):
                mine = core if half else other
                where_to = slot * mine + swapped * (1 - mine)
                piece = spread[half * chunks * rows : (half + 1) * chunks * rows]
                w_buf[:, where_to, half] = piece.reshape(chunks, rows, columns * LANES)

    barrier = pltpu.get_barrier_semaphore()
    for dev in (sib, dev_a, dev_b, dev_d):
        pl.semaphore_signal(barrier, inc=1, device_id=dev, device_id_type=MESH)
    for step in range(1, n_z):
        target = (zed + step) % n_z
        pl.semaphore_signal(
            barrier, inc=1, device_id=(seq, target * 2 + core), device_id_type=MESH
        )
    for k in range(chunks):
        load_own(k).start()
    for copy in weight_copies:
        copy.start()
    for k in range(chunks):
        load_own(k).wait()
        norm_own(k)
        if k == 0:
            pl.semaphore_wait(barrier, 4 + n_z - 1)
        own_a(k).start()
        own_b(k).start()
        own_sib(k, core).start()
        if k == 0:
            list_own()
            list_copy(A, dev_a).start()
            list_copy(B, dev_b).start()
            list_copy(DIAG, dev_d).start()
    spread_weights()

    def unit(load, load_weight, store, span, hooks):
        hidden = columns * inner
        group = 256 if hidden % 256 == 0 else LANES
        x = load()
        for first in range(0, hidden, group):
            g = dot_nt(x, gate_w[first : first + group])
            u = dot_nt(x, up_w[first : first + group])
            h = silu(g) * u
            for at in range(0, group, LANES):
                weight = load_weight((first + at) // inner)
                hid[:span, first + at : first + at + LANES] = (h[:, at : at + LANES] * weight).astype(jnp.bfloat16)
            if hooks:
                hooks.pop(0)()
        for hook in hooks:
            hook()
        tile = width // 2

        @pl.loop(0, width // tile)
        def _(n):
            cols = pl.ds(pl.multiple_of(n * tile, tile), tile)
            store(cols, jnp.dot(hid[:span], down_w[:, cols], preferred_element_type=jnp.float32).astype(jnp.bfloat16))

    def unit_at(ks, slots, count, *hooks):
        span = count * 2 * rows

        def load():
            return x_buf[ks, slots].reshape(span, width)

        def load_weight(i):
            return w_buf[ks, slots, :, :, i * LANES : (i + 1) * LANES].reshape(span, LANES)

        def store(cols, value):
            part[ks, slots, :, :, cols] = value.reshape(count, 2, rows, value.shape[-1])

        unit(load, load_weight, store, span, list(hooks))

    def shared_rows(ks, slots, span, lead):
        shape = (*lead, span.size)
        count = math.prod(shape)
        x = x_buf[ks, slots, core, span].reshape(count, width)
        shid[:count] = (silu(dot_nt(x, sgate_w[...])) * dot_nt(x, sup_w[...])).astype(jnp.bfloat16)
        tile = width // 4

        @pl.loop(0, width // tile)
        def _(n):
            cols = pl.ds(pl.multiple_of(n * tile, tile), tile)
            p = jnp.dot(shid[:count], sdown_w[:, cols], preferred_element_type=jnp.float32)
            old = part[ks, slots, core, span, cols].astype(jnp.float32)
            part[ks, slots, core, span, cols] = (old + p.reshape(*shape, tile)).astype(jnp.bfloat16)

    def shared(slot, j):
        if n_z == 4:

            @pl.when(zed == slot)
            def _():
                shared_rows(pl.ds(j * pair, pair), zed, pl.ds(0, rows), (pair,))
        else:
            mine = pl.ds(pl.multiple_of(zed * rows_z, rows_z), rows_z)
            shared_rows(pl.ds(j * pair, pair), slot, mine, (pair,))

    def add_pair(k, slot):
        part_copy(k, slot).wait_recv()
        total = part[k, slot, core].astype(jnp.float32) + from_sib[k, slot].astype(jnp.float32)
        part[k, slot, core] = total.astype(jnp.bfloat16)

    def ring_two(k):
        ring_d(k).wait_recv()
        total = part[k, B, core].astype(jnp.float32) + ring_in[k, 0].astype(jnp.float32)
        part[k, B, core] = total.astype(jnp.bfloat16)
        ring_b(k).start()

    def ring_three(k):
        ring_a(k).wait_recv()
        ring_b(k).wait_recv()
        total = (
            part[k, OWN, core].astype(jnp.float32)
            + ring_in[k, 1].astype(jnp.float32)
            + ring_in[k, 2].astype(jnp.float32)
        )
        part[k, OWN, core] = total.astype(jnp.bfloat16)
        for step in range(1, n_z):
            z_copy(k, zed, (zed + step) % n_z).start()

    def finish(k):
        total = part[
            k, OWN, core, pl.ds(pl.multiple_of(zed * rows_z, rows_z), rows_z)
        ].astype(jnp.float32)
        for step in range(1, n_z):
            source = (zed + step) % n_z
            z_copy(k, source, source).wait_recv()
            total = total + z_in[k, source].astype(jnp.float32)
        out_ref[k] = total.astype(jnp.bfloat16)

    def service(k):
        net(k, B).wait_recv()
        relay(k).start()
        over_z(k, B).start()
        sib_net(k, B, core).start()
        got_net(k, A)

    def pass_z(k):
        got_z(k, B)
        got_z(k, A)

    def send_a(k):
        add_pair(k, A)
        ring_a(k).start()
        add_pair(k, B)

    def send_d(k):
        add_pair(k, DIAG)
        ring_d(k).start()
        add_pair(k, OWN)

    for copy in weight_copies:
        copy.wait()

    def nothing():
        pass

    def when(condition, do, *args):
        @pl.when(condition)
        def _():
            do(*args)

    @pl.loop(0, pairs)
    def _(j):
        for k in range(pair):
            own_sib(j * pair + k, other).wait_recv()
        unit_at(pl.ds(j * pair, pair), OWN, pair, nothing, partial(service, j))
        for k in range(pair):
            part_copy(j * pair + k, OWN).start()
        shared(OWN, j)

    for k in range(pairs, pair):
        service(k)
    pass_z(0)

    @pl.loop(0, chunks)
    def _(k):
        for slot in (B, A):
            got_sib(k, slot)

        def early():
            when(k > 1, got_z, k - 2, DIAG)

        def middle():
            when(k + 2 < chunks, service, k + 2)

        def late():
            when(k + 1 < chunks, pass_z, k + 1)
            when(k > 0, got_net, k - 1, DIAG)

        if chunks > 1:
            unit_at(k, pl.ds(A, 2), 2, early, middle, late)
        else:
            unit_at(k, pl.ds(A, 1), 1, early, middle, late)
            unit_at(k, pl.ds(B, 1), 1)
        for slot in (A, B):
            part_copy(k, slot).start()

        @pl.when(k % pair == pair - 1)
        def _():
            shared(A, k // pair)
            shared(B, k // pair)

        when(k > 0, send_a, k - 1)

    got_net(chunks - 1, DIAG)
    if chunks > 1:
        got_z(chunks - 2, DIAG)
    if pairs == 1:
        got_z(chunks - 1, DIAG)
    send_a(chunks - 1)

    @pl.loop(0, pairs)
    def _(j):
        for k in range(pair):
            got_sib(j * pair + k, DIAG)

        def early():
            if pairs > 1:
                when(j == 0, got_z, chunks - 1, DIAG)

        unit_at(pl.ds(j * pair, pair), DIAG, pair, nothing, early)
        for k in range(pair):
            part_copy(j * pair + k, DIAG).start()
        shared(DIAG, j)
        for k in range(pair):
            when(j > 0, ring_two, (j - 1) * pair + k)
        for k in range(pair):
            send_d(j * pair + k)

    late = chunks - pair
    for k in range(pair):
        if late:
            ring_three(late - pair + k)
        ring_two(late + k)
    for k in range(pair):
        ring_three(late + k)

    for slot, dev in ((A, dev_a), (B, dev_b), (DIAG, dev_d)):
        list_copy(slot, dev).wait_send()

    @pl.loop(0, chunks)
    def _(k):
        finish(k)
        own_sib(k, core).wait_send()
        own_a(k).wait_send()
        own_b(k).wait_send()
        relay(k).wait_send()
        for slot in (A, B, DIAG):
            over_z(k, slot).wait_send()
            sib_net(k, slot, core).wait_send()
            sib_z(k, slot, core).wait_send()
        for slot in range(4):
            part_copy(k, slot).wait_send()
        ring_d(k).wait_send()
        ring_a(k).wait_send()
        ring_b(k).wait_send()
        for step in range(1, n_z):
            z_copy(k, zed, (zed + step) % n_z).wait_send()


def on_device(
    tokens,
    expert_ids,
    gate_weights,
    live,
    norm_gain,
    expert_gate,
    expert_up,
    expert_down,
    shared_gate,
    shared_up,
    shared_down,
):
    tok_seq, width = tokens.shape
    columns, inner = expert_gate.shape[:2]
    s_inner = shared_gate.shape[0]
    n_seq = lax.axis_size("seq")
    n_tp = lax.axis_size("tp")
    assert n_seq == 4
    tok_dev = tok_seq // n_tp
    n_z = n_tp // 2
    chunks = max(1, min(4, tok_dev // 16))
    rows_z = tok_dev // chunks
    rows = n_z * rows_z
    assert rows_z & (rows_z - 1) == 0 and chunks & (chunks - 1) == 0
    experts = columns * n_tp
    listed = -(-experts // 16) * 16
    share = width * 5 // 20 // LANES * LANES
    pair = min(2, chunks)
    hid_rows = 2 * rows * pair
    shared_take = pair * (rows if n_z == 4 else rows_z)

    bf16 = jnp.bfloat16
    dma = pltpu.SemaphoreType.DMA
    vmem = pl.BlockSpec(memory_space=pltpu.VMEM)
    out = pl.pallas_call(
        partial(layer_kernel, chunks, n_z, columns, width, rows_z, share),
        out_shape=jax.ShapeDtypeStruct((chunks, rows_z, width), bf16),
        in_specs=[pl.BlockSpec(memory_space=pl.ANY), vmem, vmem, vmem, vmem]
        + [pl.BlockSpec(memory_space=pl.ANY)] * 6,
        out_specs=vmem,
        scratch_shapes=[
            pltpu.VMEM((chunks, 4, 2, rows, width), bf16),
            pltpu.VMEM((chunks, 4, 2, rows, width), bf16),
            pltpu.VMEM((chunks, 4, rows, width), bf16),
            pltpu.VMEM((chunks, 3, rows, width), bf16),
            pltpu.VMEM((chunks, n_z, rows_z, width), bf16),
            pltpu.VMEM((columns * inner, width), bf16),
            pltpu.VMEM((columns * inner, width), bf16),
            pltpu.VMEM((columns * inner, width), bf16),
            pltpu.VMEM((s_inner, width), bf16),
            pltpu.VMEM((s_inner, width), bf16),
            pltpu.VMEM((s_inner, width), bf16),
            pltpu.VMEM((hid_rows, columns * inner), bf16),
            pltpu.VMEM((shared_take, s_inner), bf16),
            pltpu.VMEM((chunks, n_z, rows_z, width), bf16),
            pltpu.VMEM((4, listed, tok_seq), bf16),
            pltpu.VMEM((chunks, 4, 2, rows, columns * LANES), jnp.float32),
            dma((6,)),
            dma((chunks,)),
            dma((3,)),
            dma((chunks, 3)),
            dma((chunks, 10)),
            dma((chunks, 4)),
            dma((chunks, 3)),
            dma((chunks, n_z)),
            dma((3,)),
            dma((chunks, 4, 4)),
            dma((chunks, 4)),
            dma((chunks, 3)),
            dma((chunks, n_z)),
        ],
        compiler_params=pltpu.CompilerParams(
            collective_id=0, has_side_effects=True, vmem_limit_bytes=62 * 1024 * 1024
        ),
    )(
        tokens.reshape(n_z, 2, chunks, rows_z, width),
        norm_gain,
        expert_ids.T,
        gate_weights.T,
        live,
        expert_gate.reshape(columns * inner, width),
        expert_up.reshape(columns * inner, width),
        expert_down.reshape(columns * inner, width),
        shared_gate,
        shared_up,
        shared_down,
    )
    return out.reshape(tok_dev, width)


def solution(mesh):
    placed = (
        P("seq", None),
        P("seq", None),
        P("seq", None),
        P("seq"),
        P(),
        P("tp", "seq", None),
        P("tp", "seq", None),
        P("tp", "seq", None),
        P("seq", None),
        P("seq", None),
        P("seq", None),
    )
    return jax.shard_map(
        on_device, mesh=mesh, in_specs=placed, out_specs=P(("seq", "tp"), None), check_vma=False
    )
```

```python
import math
from functools import partial

import jax
import jax.numpy as jnp
from jax import lax
from jax.experimental import pallas as pl
from jax.experimental.pallas import tpu as pltpu
from jax.sharding import PartitionSpec as P

MESH = pl.DeviceIdType.MESH
LANES = 128
OWN, A, B, DIAG = 0, 1, 2, 3
UNITS = (
    ((OWN, 0), (OWN, 1)),
    ((OWN, 2), (OWN, 3)),
    ((A, 0), (B, 0)),
    ((A, 1), (B, 1)),
    ((DIAG, 0), (DIAG, 1)),
    ((A, 2), (B, 2)),
    ((A, 3), (B, 3)),
    ((DIAG, 2), (DIAG, 3)),
)
UNITS_ONE = (((OWN, 0),), ((A, 0),), ((B, 0),), ((DIAG, 0),))
STEPS = {
    (0, 0): (("take_a", 0),),
    (0, 1): (("take_b", 0),),
    (1, 1): (("take_b", 1),),
    (1, 2): (("own", 2),),
    (1, 3): (("take_a", 1), ("pair_own", 1), ("pass_z", 0),),
    (2, 0): (("take_d", 0), ("own", 3),),
    (2, 1): (("take_d", 1),),
    (2, 2): (("pair_own", 3), ("pair_own", 0),),
    (2, 3): (("take_b", 2), ("pass_z", 1),),
    (3, 1): (("take_a", 2),),
    (3, 2): (("take_b", 3),),
    (3, 3): (("pass_d", 0),),
    (4, 0): (("pass_d", 1), ("ring_a", 1), ("ring_a", 0), ("take_a", 3),),
    (4, 2): (("pair_own", 2),),
    (4, 3): (("pass_z", 2),),
    (4, 4): (("take_d", 3),),
    (5, 1): (("take_d", 2),),
    (5, 2): (("pair_b", 1), ("ring_d", 1),),
    (5, 3): (("ring_d", 0), ("pass_z", 3),),
    (6, 3): (("ring_b", 1), ("pair_b", 0), ("pair_b", 2), ("pass_d", 3),),
    (6, 4): (("ring_a", 2),),
    (7, 0): (("pass_d", 2), ("ring_b", 0),),
    (7, 4): (("over_z", 1), ("pair_b", 3),),
    (8, 0): (("ring_d", 2), ("over_z", 0), ("ring_d", 3), ("ring_b", 2), ("ring_b", 3), ("ring_a", 3), ("over_z", 2), ("over_z", 3),),
}
STEPS_ONE = {
    (0, 4): (("take_b", 0), ("take_a", 0), ("pass_z", 0)),
    (1, 4): (("take_d", 0),),
    (2, 4): (("pass_d", 0), ("ring_a", 0), ("pair_b", 0)),
    (4, 0): (("ring_d", 0), ("pair_own", 0), ("ring_b", 0), ("over_z", 0)),
}


def dot_nt(a, b):
    return lax.dot_general(a, b, (((1,), (1,)), ((), ())), preferred_element_type=jnp.float32)


def silu(v):
    return v / (1.0 + jnp.exp(-v))


def layer_kernel(
    chunks,
    n_z,
    columns,
    width,
    rows_z,
    share,
    tok_hbm,
    gain_ref,
    ids_ref,
    gates_ref,
    live_ref,
    gate_hbm,
    up_hbm,
    down_hbm,
    sgate_hbm,
    sup_hbm,
    sdown_hbm,
    out_ref,
    x_buf,
    part,
    from_sib,
    ring_in,
    z_in,
    gate_w,
    up_w,
    down_w,
    sgate_w,
    sup_w,
    sdown_w,
    hid,
    shid,
    tok_v,
    lists,
    w_buf,
    w_sem,
    own_sem,
    send_list,
    send_own,
    send_fwd,
    send_part,
    send_ring,
    send_z,
    recv_list,
    recv_x,
    recv_part,
    recv_ring,
    recv_z,
):
    seq = lax.axis_index("seq")
    tp = lax.axis_index("tp")
    core = tp % 2
    zed = tp // 2
    other = 1 - core
    sx = seq % 2
    sy = seq // 2
    nbr_x = sy * 2 + (1 - sx)
    nbr_y = (1 - sy) * 2 + sx
    sib = (seq, zed * 2 + other)
    dev_a = (nbr_y * other + nbr_x * core, tp)
    dev_b = (nbr_x * other + nbr_y * core, tp)
    dev_d = (3 - seq, tp)
    rows = n_z * rows_z
    parity = zed % 2
    dev_z = (seq, (zed + 1 - 2 * parity) * 2 + core)
    fetched = pl.ds(pl.multiple_of(parity * share, LANES), width - share)
    passed = pl.ds(pl.multiple_of(parity * (width - share), LANES), share)
    given = pl.ds(pl.multiple_of((1 - parity) * (width - share), LANES), share)
    whole = pl.ds(0, width)
    inner = gate_w.shape[0] // columns
    tok_seq = ids_ref.shape[1]
    units, steps = (UNITS, STEPS) if chunks == 4 else (UNITS_ONE, STEPS_ONE)
    place = {which: (u, i) for u, unit in enumerate(units) for i, which in enumerate(unit)}
    count = len(units[0])

    def remote(src, dst, ssem, rsem, dev):
        return pltpu.make_async_remote_copy(
            src_ref=src, dst_ref=dst, send_sem=ssem, recv_sem=rsem, device_id=dev, device_id_type=MESH
        )

    def x_copy(k, src_slot, dst_slot, half, cols, ssem, kind, dev):
        return remote(
            x_buf.at[(*place[src_slot, k], half, slice(None), cols)],
            x_buf.at[(*place[dst_slot, k], half, slice(None), cols)],
            ssem,
            recv_x.at[k, dst_slot, kind],
            dev,
        )

    def own_a(k):
        return x_copy(k, OWN, A, core, fetched, send_own.at[k, 1], 0, dev_a)

    def own_b(k):
        return x_copy(k, OWN, B, core, fetched, send_own.at[k, 2], 0, dev_b)

    def own_sib(k, half):
        return x_copy(k, OWN, OWN, half, whole, send_own.at[k, 0], 2, sib)

    def net(k, slot):
        return x_copy(k, slot, slot, core, fetched, send_fwd.at[k, 0], 0, dev_a)

    def relay(k):
        return x_copy(k, B, DIAG, core, fetched, send_fwd.at[k, 0], 0, dev_a)

    def over_z(k, slot):
        return x_copy(k, slot, slot, core, passed, send_fwd.at[k, slot], 1, dev_z)

    def from_z(k, slot):
        return x_copy(k, slot, slot, core, given, send_fwd.at[k, slot], 1, dev_z)

    def sib_net(k, slot, half):
        return x_copy(k, slot, slot, half, fetched, send_fwd.at[k, slot + 3], 2, sib)

    def sib_z(k, slot, half):
        return x_copy(k, slot, slot, half, given, send_fwd.at[k, slot + 6], 3, sib)

    def got_net(k, slot):
        net(k, slot).wait_recv()
        over_z(k, slot).start()
        sib_net(k, slot, core).start()

    def got_z(k, slot):
        from_z(k, slot).wait_recv()
        sib_z(k, slot, core).start()

    def got_sib(k, slot):
        sib_net(k, slot, other).wait_recv()
        sib_z(k, slot, other).wait_recv()

    def list_copy(slot, dev):
        return remote(lists.at[OWN], lists.at[slot], send_list.at[slot - 1], recv_list.at[slot - 1], dev)

    def part_copy(u, i):
        return remote(part.at[u, i, other], from_sib.at[u, i], send_part.at[u, i], recv_part.at[u, i], sib)

    def ring_copy(k, slot, leg, dev):
        return remote(
            part.at[(*place[slot, k], core)],
            ring_in.at[k, leg],
            send_ring.at[k, leg],
            recv_ring.at[k, leg],
            dev,
        )

    def ring_d(k):
        return ring_copy(k, DIAG, 0, dev_a)

    def ring_a(k):
        return ring_copy(k, A, 1, dev_a)

    def ring_b(k):
        return ring_copy(k, B, 2, dev_b)

    def z_copy(k, src_z, dst_z):
        return remote(
            part.at[(*place[OWN, k], core, pl.ds(dst_z * rows_z, rows_z))],
            z_in.at[k, src_z],
            send_z.at[k, dst_z],
            recv_z.at[k, src_z],
            (seq, dst_z * 2 + core),
        )

    weight_copies = [
        pltpu.make_async_copy(src, dst, w_sem.at[i])
        for i, (src, dst) in enumerate(
            (
                (gate_hbm, gate_w),
                (up_hbm, up_w),
                (down_hbm, down_w),
                (sgate_hbm, sgate_w),
                (sup_hbm, sup_w),
                (sdown_hbm, sdown_w),
            )
        )
    ]

    def load_own(k):
        return pltpu.make_async_copy(tok_hbm.at[:, core, k], tok_v.at[k], own_sem.at[k])

    def norm_own(k):
        values = tok_v[k].reshape(rows, width).astype(jnp.float32)
        scale = lax.rsqrt(jnp.mean(values * values, axis=-1, keepdims=True) + 1e-05)
        gain = gain_ref[...].reshape(1, width)
        x_buf[(*place[OWN, k], core)] = (values * scale * gain).astype(jnp.bfloat16)

    def list_own():
        weight = gates_ref[...].astype(jnp.float32) * live_ref[...].reshape(1, tok_seq).astype(jnp.float32)
        expert = lax.broadcasted_iota(jnp.int32, lists.shape[1:], 0)
        total = jnp.zeros(lists.shape[1:], jnp.float32)
        for j in range(ids_ref.shape[0]):
            total = total + jnp.where(ids_ref[j : j + 1] == expert, weight[j : j + 1], 0.0)
        lists[OWN] = total.astype(jnp.bfloat16)

    def spread_weights():
        token = lax.broadcasted_iota(jnp.int32, (1, tok_seq), 1)
        bits_r = rows_z.bit_length() - 1
        bits_k = chunks.bit_length() - 1
        at_r = token & (rows_z - 1)
        at_k = (token >> bits_r) & (chunks - 1)
        at_half = (token >> (bits_r + bits_k)) & 1
        at_z = token >> (bits_r + bits_k + 1)
        spot = (at_half * chunks + at_k) * rows + at_z * rows_z + at_r
        row = lax.broadcasted_iota(jnp.int32, (tok_seq, tok_seq), 0)
        onehot = jnp.where(row == spot, 1.0, 0.0).astype(jnp.bfloat16)
        expert = lax.broadcasted_iota(jnp.int32, lists.shape[1:], 0)
        for slot in range(4):
            if slot:
                list_copy(slot, dev_a).wait_recv()
            listed = lists[slot].astype(jnp.float32)
            picked = []
            for i in range(columns):
                mine = jnp.where(expert == tp * columns + i, listed, 0.0)
                mine = jnp.sum(mine, axis=0, keepdims=True)
                picked.append(jnp.broadcast_to(mine, (LANES, tok_seq)))
            spread = dot_nt(onehot, jnp.concatenate(picked, axis=0).astype(jnp.bfloat16))
            swapped = {OWN: OWN, A: B, B: A, DIAG: DIAG}[slot]
            for half in range(2):
                mine = core if half else other
                for k in range(chunks):
                    u, i = (p * mine + q * (1 - mine) for p, q in zip(place[slot, k], place[swapped, k]))
                    first = (half * chunks + k) * rows
                    w_buf[u, i, half] = spread[first : first + rows]

    barrier = pltpu.get_barrier_semaphore()
    for dev in (sib, dev_a, dev_b, dev_d):
        pl.semaphore_signal(barrier, inc=1, device_id=dev, device_id_type=MESH)
    for step in range(1, n_z):
        target = (zed + step) % n_z
        pl.semaphore_signal(
            barrier, inc=1, device_id=(seq, target * 2 + core), device_id_type=MESH
        )
    for k in range(chunks):
        load_own(k).start()
    for copy in weight_copies:
        copy.start()
    for k in range(chunks):
        load_own(k).wait()
        norm_own(k)
        if k == 0:
            pl.semaphore_wait(barrier, 4 + n_z - 1)
        if k < 2:
            own_a(k).start()
            own_b(k).start()
        own_sib(k, core).start()
        if k == 0:
            list_own()
            list_copy(A, dev_a).start()
            list_copy(B, dev_b).start()
            list_copy(DIAG, dev_d).start()
    spread_weights()

    def unit(u):
        span = count * 2 * rows
        hidden = columns * inner
        group = hidden // 3
        for n in range(3):
            first = n * group
            x = x_buf[u].reshape(span, width)
            g = dot_nt(x, gate_w[first : first + group])
            up = dot_nt(x, up_w[first : first + group])
            h = silu(g) * up
            for at in range(0, group, LANES):
                i = (first + at) // inner
                weight = w_buf[u, :, :, :, i * LANES : (i + 1) * LANES].reshape(span, LANES)
                hid[:, first + at : first + at + LANES] = (h[:, at : at + LANES] * weight).astype(jnp.bfloat16)
            do(u, n + 1)
        tile = width // 2

        @pl.loop(0, width // tile)
        def _(n):
            cols = pl.ds(pl.multiple_of(n * tile, tile), tile)
            p = jnp.dot(hid[...], down_w[:, cols], preferred_element_type=jnp.float32)
            part[u, :, :, :, cols] = p.astype(jnp.bfloat16).reshape(count, 2, rows, tile)

    def shared_rows(pieces, span):
        take = span.size
        total = len(pieces) * take
        x = jnp.concatenate([x_buf[u, i, core, span] for u, i in pieces], axis=0)
        shid[:total] = (silu(dot_nt(x, sgate_w[...])) * dot_nt(x, sup_w[...])).astype(jnp.bfloat16)
        tile = width // 4

        @pl.loop(0, width // tile)
        def _(n):
            cols = pl.ds(pl.multiple_of(n * tile, tile), tile)
            p = jnp.dot(shid[:total], sdown_w[:, cols], preferred_element_type=jnp.float32)
            for at, (u, i) in enumerate(pieces):
                old = part[u, i, core, span, cols].astype(jnp.float32)
                part[u, i, core, span, cols] = (old + p[at * take : (at + 1) * take]).astype(jnp.bfloat16)

    def among(u, those):
        found = u == those[0]
        for other_unit in those[1:]:
            found = jnp.logical_or(found, u == other_unit)
        return found

    def shared(u):
        if n_z == 4 and chunks == 4:
            every = pl.ds(0, rows)
            owns = [place[OWN, k][0] for k in (0, 2)]
            diags = [place[DIAG, k][0] for k in (0, 2)]
            mixed = [place[A, k][0] for k in (1, 3)]
            is_own = jnp.logical_and(zed == OWN, among(u, owns))
            is_diag = jnp.logical_and(zed == DIAG, among(u, diags))

            @pl.when(jnp.logical_or(is_own, is_diag))
            def _():
                shared_rows([(u, 0), (u, 1)], every)

            @pl.when(jnp.logical_and(jnp.logical_or(zed == A, zed == B), among(u, mixed)))
            def _():
                shared_rows([(u - 1, zed - 1), (u, zed - 1)], every)
        else:
            mine = pl.ds(pl.multiple_of(zed * rows_z, rows_z), rows_z)
            shared_rows([(u, i) for i in range(count)], mine)

    def add_up(at, *terms):
        @pl.loop(0, rows // 16)
        def _(n):
            some = pl.ds(pl.multiple_of(n * 16, 16), 16)
            total = part[(*at, core, some)].astype(jnp.float32)
            for ref, index in terms:
                total = total + ref[(*index, some)].astype(jnp.float32)
            part[(*at, core, some)] = total.astype(jnp.bfloat16)

    def add_pair(k, slot):
        at = place[slot, k]
        part_copy(*at).wait_recv()
        add_up(at, (from_sib, at))

    def step_own(k):
        own_a(k).start()
        own_b(k).start()

    def step_take_b(k):
        net(k, B).wait_recv()
        relay(k).start()
        over_z(k, B).start()
        sib_net(k, B, core).start()

    def step_take_a(k):
        got_net(k, A)

    def step_take_d(k):
        got_net(k, DIAG)

    def step_pass_z(k):
        got_z(k, B)
        got_z(k, A)

    def step_pass_d(k):
        got_z(k, DIAG)

    def step_ring_a(k):
        add_pair(k, A)
        ring_a(k).start()

    def step_pair_b(k):
        add_pair(k, B)

    def step_ring_d(k):
        add_pair(k, DIAG)
        ring_d(k).start()

    def step_pair_own(k):
        add_pair(k, OWN)

    def step_ring_b(k):
        ring_d(k).wait_recv()
        add_up(place[B, k], (ring_in, (k, 0)))
        ring_b(k).start()

    def step_over_z(k):
        ring_a(k).wait_recv()
        ring_b(k).wait_recv()
        add_up(place[OWN, k], (ring_in, (k, 1)), (ring_in, (k, 2)))
        for step in range(1, n_z):
            z_copy(k, zed, (zed + step) % n_z).start()

    actions = {
        "own": step_own,
        "take_b": step_take_b,
        "take_a": step_take_a,
        "take_d": step_take_d,
        "pass_z": step_pass_z,
        "pass_d": step_pass_d,
        "ring_a": step_ring_a,
        "pair_b": step_pair_b,
        "ring_d": step_ring_d,
        "pair_own": step_pair_own,
        "ring_b": step_ring_b,
        "over_z": step_over_z,
    }

    def run(at):
        for name, k in steps.get(at, ()):
            actions[name](k)

    def do(u, point):
        for n in range(len(units)):
            if (n, point) in steps:

                @pl.when(u == n)
                def _():
                    run((n, point))

    def finish(k):
        mine = pl.ds(pl.multiple_of(zed * rows_z, rows_z), rows_z)
        total = part[(*place[OWN, k], core, mine)].astype(jnp.float32)
        for step in range(1, n_z):
            source = (zed + step) % n_z
            z_copy(k, source, source).wait_recv()
            total = total + z_in[k, source].astype(jnp.float32)
        out_ref[k] = total.astype(jnp.bfloat16)

    for copy in weight_copies:
        copy.wait()

    def ready(n):
        for slot, k in units[n]:
            if slot == OWN:
                own_sib(k, other).wait_recv()
            else:
                got_sib(k, slot)

    @pl.loop(0, len(units))
    def _(u):
        do(u, 0)
        for n in range(len(units)):

            @pl.when(u == n)
            def _():
                ready(n)

        unit(u)
        for i in range(count):
            part_copy(u, i).start()
        shared(u)
        do(u, 4)

    run((len(units), 0))

    for slot, dev in ((A, dev_a), (B, dev_b), (DIAG, dev_d)):
        list_copy(slot, dev).wait_send()

    for k in range(chunks):
        finish(k)
    for k in range(chunks):
        own_sib(k, core).wait_send()
        own_a(k).wait_send()
        own_b(k).wait_send()
        relay(k).wait_send()
        for slot in (A, B, DIAG):
            over_z(k, slot).wait_send()
            sib_net(k, slot, core).wait_send()
            sib_z(k, slot, core).wait_send()
        ring_d(k).wait_send()
        ring_a(k).wait_send()
        ring_b(k).wait_send()
        for step in range(1, n_z):
            z_copy(k, zed, (zed + step) % n_z).wait_send()
    for u in range(len(units)):
        for i in range(count):
            part_copy(u, i).wait_send()


def on_device(
    tokens,
    expert_ids,
    gate_weights,
    live,
    norm_gain,
    expert_gate,
    expert_up,
    expert_down,
    shared_gate,
    shared_up,
    shared_down,
):
    tok_seq, width = tokens.shape
    columns, inner = expert_gate.shape[:2]
    s_inner = shared_gate.shape[0]
    n_seq = lax.axis_size("seq")
    n_tp = lax.axis_size("tp")
    assert n_seq == 4
    tok_dev = tok_seq // n_tp
    n_z = n_tp // 2
    chunks = 4 if tok_dev >= 64 else 1
    rows_z = tok_dev // chunks
    rows = n_z * rows_z
    assert rows_z & (rows_z - 1) == 0 and chunks & (chunks - 1) == 0
    experts = columns * n_tp
    listed = -(-experts // 16) * 16
    share = width * 8 // 20 // LANES * LANES
    n_units, count = (len(UNITS), 2) if chunks == 4 else (len(UNITS_ONE), 1)

    bf16 = jnp.bfloat16
    dma = pltpu.SemaphoreType.DMA
    vmem = pl.BlockSpec(memory_space=pltpu.VMEM)
    out = pl.pallas_call(
        partial(layer_kernel, chunks, n_z, columns, width, rows_z, share),
        out_shape=jax.ShapeDtypeStruct((chunks, rows_z, width), bf16),
        in_specs=[pl.BlockSpec(memory_space=pl.ANY), vmem, vmem, vmem, vmem]
        + [pl.BlockSpec(memory_space=pl.ANY)] * 6,
        out_specs=vmem,
        scratch_shapes=[
            pltpu.VMEM((n_units, count, 2, rows, width), bf16),
            pltpu.VMEM((n_units, count, 2, rows, width), bf16),
            pltpu.VMEM((n_units, count, rows, width), bf16),
            pltpu.VMEM((chunks, 3, rows, width), bf16),
            pltpu.VMEM((chunks, n_z, rows_z, width), bf16),
            pltpu.VMEM((columns * inner, width), bf16),
            pltpu.VMEM((columns * inner, width), bf16),
            pltpu.VMEM((columns * inner, width), bf16),
            pltpu.VMEM((s_inner, width), bf16),
            pltpu.VMEM((s_inner, width), bf16),
            pltpu.VMEM((s_inner, width), bf16),
            pltpu.VMEM((count * 2 * rows, columns * inner), bf16),
            pltpu.VMEM((2 * rows, s_inner), bf16),
            pltpu.VMEM((chunks, n_z, rows_z, width), bf16),
            pltpu.VMEM((4, listed, tok_seq), bf16),
            pltpu.VMEM((n_units, count, 2, rows, columns * LANES), jnp.float32),
            dma((6,)),
            dma((chunks,)),
            dma((3,)),
            dma((chunks, 3)),
            dma((chunks, 10)),
            dma((n_units, count)),
            dma((chunks, 3)),
            dma((chunks, n_z)),
            dma((3,)),
            dma((chunks, 4, 4)),
            dma((n_units, count)),
            dma((chunks, 3)),
            dma((chunks, n_z)),
        ],
        compiler_params=pltpu.CompilerParams(
            collective_id=0, has_side_effects=True, vmem_limit_bytes=62 * 1024 * 1024
        ),
    )(
        tokens.reshape(n_z, 2, chunks, rows_z, width),
        norm_gain,
        expert_ids.T,
        gate_weights.T,
        live,
        expert_gate.reshape(columns * inner, width),
        expert_up.reshape(columns * inner, width),
        expert_down.reshape(columns * inner, width),
        shared_gate,
        shared_up,
        shared_down,
    )
    return out.reshape(tok_dev, width)


def solution(mesh):
    placed = (
        P("seq", None),
        P("seq", None),
        P("seq", None),
        P("seq"),
        P(),
        P("tp", "seq", None),
        P("tp", "seq", None),
        P("tp", "seq", None),
        P("seq", None),
        P("seq", None),
        P("seq", None),
    )
    return jax.shard_map(
        on_device, mesh=mesh, in_specs=placed, out_specs=P(("seq", "tp"), None), check_vma=False
    )
```

```python
import math
from functools import partial

import jax
import jax.numpy as jnp
from jax import lax
from jax.experimental import pallas as pl
from jax.experimental.pallas import tpu as pltpu
from jax.sharding import PartitionSpec as P

MESH = pl.DeviceIdType.MESH
LANES = 128
OWN, A, B, DIAG = 0, 1, 2, 3
UNITS = (
    ((OWN, 0), (OWN, 1)),
    ((OWN, 2), (OWN, 3)),
    ((A, 0), (B, 0)),
    ((A, 1), (B, 1)),
    ((DIAG, 0), (DIAG, 1)),
    ((A, 2), (B, 2)),
    ((A, 3), (B, 3)),
    ((DIAG, 2), (DIAG, 3)),
)
UNITS_ONE = (((OWN, 0),), ((A, 0),), ((B, 0),), ((DIAG, 0),))
STEPS = {
    (0, 0): (("take_a", 0),),
    (0, 1): (("take_b", 0),),
    (1, 1): (("take_b", 1),),
    (1, 2): (("own", 2),),
    (1, 3): (("take_a", 1), ("pair_own", 1), ("pass_z", 0),),
    (2, 0): (("take_d", 0), ("own", 3),),
    (2, 1): (("take_d", 1),),
    (2, 2): (("pair_own", 3), ("pair_own", 0),),
    (2, 3): (("take_b", 2), ("pass_z", 1),),
    (3, 1): (("take_a", 2),),
    (3, 2): (("take_b", 3),),
    (3, 3): (("pass_d", 0),),
    (4, 0): (("pass_d", 1), ("ring_a", 1), ("ring_a", 0), ("take_a", 3),),
    (4, 2): (("pair_own", 2),),
    (4, 3): (("pass_z", 2),),
    (4, 5): (("take_d", 3),),
    (5, 1): (("take_d", 2),),
    (5, 2): (("pair_b", 1), ("ring_d", 1),),
    (5, 3): (("ring_d", 0), ("pass_z", 3),),
    (6, 3): (("ring_b", 1), ("pair_b", 0), ("pair_b", 2), ("pass_d", 3),),
    (6, 5): (("ring_a", 2),),
    (7, 0): (("pass_d", 2), ("ring_b", 0),),
    (7, 5): (("over_z", 1), ("pair_b", 3),),
    (8, 0): (("ring_d", 2), ("over_z", 0), ("ring_d", 3), ("ring_b", 2), ("ring_b", 3), ("ring_a", 3), ("over_z", 2), ("over_z", 3),),
}
SHARES = ((8, 8), (8, 8), (8, 8), (8, 8))
SHARES_ONE = ((5, 5),)
STEPS_ONE = {
    (0, 5): (("take_b", 0), ("take_a", 0), ("pass_z", 0)),
    (1, 5): (("take_d", 0),),
    (2, 5): (("pass_d", 0), ("ring_a", 0), ("pair_b", 0)),
    (4, 0): (("ring_d", 0), ("pair_own", 0), ("ring_b", 0), ("over_z", 0)),
}


def dot_nt(a, b):
    return lax.dot_general(a, b, (((1,), (1,)), ((), ())), preferred_element_type=jnp.float32)


def silu(v):
    return v / (1.0 + jnp.exp(-v))


def layer_kernel(
    chunks,
    n_z,
    columns,
    width,
    rows_z,
    tok_hbm,
    gain_ref,
    ids_ref,
    gates_ref,
    live_ref,
    gate_hbm,
    up_hbm,
    down_hbm,
    sgate_hbm,
    sup_hbm,
    sdown_hbm,
    out_ref,
    x_buf,
    part,
    from_sib,
    ring_in,
    z_in,
    gate_w,
    up_w,
    down_w,
    sgate_w,
    sup_w,
    sdown_w,
    hid,
    shid,
    tok_v,
    lists,
    w_buf,
    w_sem,
    own_sem,
    send_list,
    send_own,
    send_fwd,
    send_part,
    send_ring,
    send_z,
    recv_list,
    recv_x,
    recv_part,
    recv_ring,
    recv_z,
):
    seq = lax.axis_index("seq")
    tp = lax.axis_index("tp")
    core = tp % 2
    zed = tp // 2
    other = 1 - core
    sx = seq % 2
    sy = seq // 2
    nbr_x = sy * 2 + (1 - sx)
    nbr_y = (1 - sy) * 2 + sx
    sib = (seq, zed * 2 + other)
    dev_a = (nbr_y * other + nbr_x * core, tp)
    dev_b = (nbr_x * other + nbr_y * core, tp)
    dev_d = (3 - seq, tp)
    rows = n_z * rows_z
    parity = zed % 2
    dev_z = (seq, (zed + 1 - 2 * parity) * 2 + core)
    def share_of(k, slot):
        return width * shares[k][slot == DIAG] // 20 // LANES * LANES

    def fetched(k, slot):
        share = share_of(k, slot)
        return pl.ds(pl.multiple_of(parity * share, LANES), width - share)

    def passed(k, slot):
        share = share_of(k, slot)
        return pl.ds(pl.multiple_of(parity * (width - share), LANES), share)

    def given(k, slot):
        share = share_of(k, slot)
        return pl.ds(pl.multiple_of((1 - parity) * (width - share), LANES), share)

    whole = pl.ds(0, width)
    inner = gate_w.shape[0] // columns
    tok_seq = ids_ref.shape[1]
    units, steps, shares = (UNITS, STEPS, SHARES) if chunks == 4 else (UNITS_ONE, STEPS_ONE, SHARES_ONE)
    place = {which: (u, i) for u, unit in enumerate(units) for i, which in enumerate(unit)}
    count = len(units[0])

    def remote(src, dst, ssem, rsem, dev):
        return pltpu.make_async_remote_copy(
            src_ref=src, dst_ref=dst, send_sem=ssem, recv_sem=rsem, device_id=dev, device_id_type=MESH
        )

    def x_copy(k, src_slot, dst_slot, half, cols, ssem, kind, dev):
        return remote(
            x_buf.at[(*place[src_slot, k], half, slice(None), cols)],
            x_buf.at[(*place[dst_slot, k], half, slice(None), cols)],
            ssem,
            recv_x.at[k, dst_slot, kind],
            dev,
        )

    def own_a(k):
        return x_copy(k, OWN, A, core, fetched(k, A), send_own.at[k, 1], 0, dev_a)

    def own_b(k):
        return x_copy(k, OWN, B, core, fetched(k, B), send_own.at[k, 2], 0, dev_b)

    def own_sib(k, half):
        return x_copy(k, OWN, OWN, half, whole, send_own.at[k, 0], 2, sib)

    def net(k, slot):
        return x_copy(k, slot, slot, core, fetched(k, slot), send_fwd.at[k, 0], 0, dev_a)

    def relay(k):
        return x_copy(k, B, DIAG, core, fetched(k, DIAG), send_fwd.at[k, 0], 0, dev_a)

    def over_z(k, slot):
        return x_copy(k, slot, slot, core, passed(k, slot), send_fwd.at[k, slot], 1, dev_z)

    def from_z(k, slot):
        return x_copy(k, slot, slot, core, given(k, slot), send_fwd.at[k, slot], 1, dev_z)

    def sib_net(k, slot, half):
        return x_copy(k, slot, slot, half, fetched(k, slot), send_fwd.at[k, slot + 3], 2, sib)

    def sib_z(k, slot, half):
        return x_copy(k, slot, slot, half, given(k, slot), send_fwd.at[k, slot + 6], 3, sib)

    def got_net(k, slot):
        net(k, slot).wait_recv()
        over_z(k, slot).start()
        sib_net(k, slot, core).start()

    def got_z(k, slot):
        from_z(k, slot).wait_recv()
        sib_z(k, slot, core).start()

    def got_sib(k, slot):
        sib_net(k, slot, other).wait_recv()
        sib_z(k, slot, other).wait_recv()

    def list_copy(slot, dev):
        return remote(lists.at[OWN], lists.at[slot], send_list.at[slot - 1], recv_list.at[slot - 1], dev)

    def part_copy(u, i):
        return remote(part.at[u, i, other], from_sib.at[u, i], send_part.at[u, i], recv_part.at[u, i], sib)

    def ring_copy(k, slot, leg, dev):
        return remote(
            part.at[(*place[slot, k], core)],
            ring_in.at[k, leg],
            send_ring.at[k, leg],
            recv_ring.at[k, leg],
            dev,
        )

    def ring_d(k):
        return ring_copy(k, DIAG, 0, dev_a)

    def ring_a(k):
        return ring_copy(k, A, 1, dev_a)

    def ring_b(k):
        return ring_copy(k, B, 2, dev_b)

    def z_copy(k, src_z, dst_z):
        return remote(
            part.at[(*place[OWN, k], core, pl.ds(dst_z * rows_z, rows_z))],
            z_in.at[k, src_z],
            send_z.at[k, dst_z],
            recv_z.at[k, src_z],
            (seq, dst_z * 2 + core),
        )

    weight_copies = [
        pltpu.make_async_copy(src, dst, w_sem.at[i])
        for i, (src, dst) in enumerate(
            (
                (gate_hbm, gate_w),
                (up_hbm, up_w),
                (down_hbm, down_w),
                (sgate_hbm, sgate_w),
                (sup_hbm, sup_w),
                (sdown_hbm, sdown_w),
            )
        )
    ]

    def load_own(k):
        return pltpu.make_async_copy(tok_hbm.at[:, core, k], tok_v.at[k], own_sem.at[k])

    def norm_own(k):
        values = tok_v[k].reshape(rows, width).astype(jnp.float32)
        scale = lax.rsqrt(jnp.mean(values * values, axis=-1, keepdims=True) + 1e-05)
        gain = gain_ref[...].reshape(1, width)
        x_buf[(*place[OWN, k], core)] = (values * scale * gain).astype(jnp.bfloat16)

    def list_own():
        weight = gates_ref[...].astype(jnp.float32) * live_ref[...].reshape(1, tok_seq).astype(jnp.float32)
        expert = lax.broadcasted_iota(jnp.int32, lists.shape[1:], 0)
        total = jnp.zeros(lists.shape[1:], jnp.float32)
        for j in range(ids_ref.shape[0]):
            total = total + jnp.where(ids_ref[j : j + 1] == expert, weight[j : j + 1], 0.0)
        lists[OWN] = total.astype(jnp.bfloat16)

    def spread_weights():
        token = lax.broadcasted_iota(jnp.int32, (1, tok_seq), 1)
        bits_r = rows_z.bit_length() - 1
        bits_k = chunks.bit_length() - 1
        at_r = token & (rows_z - 1)
        at_k = (token >> bits_r) & (chunks - 1)
        at_half = (token >> (bits_r + bits_k)) & 1
        at_z = token >> (bits_r + bits_k + 1)
        spot = (at_half * chunks + at_k) * rows + at_z * rows_z + at_r
        row = lax.broadcasted_iota(jnp.int32, (tok_seq, tok_seq), 0)
        onehot = jnp.where(row == spot, 1.0, 0.0).astype(jnp.bfloat16)
        expert = lax.broadcasted_iota(jnp.int32, lists.shape[1:], 0)
        for slot in range(4):
            if slot:
                list_copy(slot, dev_a).wait_recv()
            listed = lists[slot].astype(jnp.float32)
            picked = []
            for i in range(columns):
                mine = jnp.where(expert == tp * columns + i, listed, 0.0)
                mine = jnp.sum(mine, axis=0, keepdims=True)
                picked.append(jnp.broadcast_to(mine, (LANES, tok_seq)))
            spread = dot_nt(onehot, jnp.concatenate(picked, axis=0).astype(jnp.bfloat16))
            swapped = {OWN: OWN, A: B, B: A, DIAG: DIAG}[slot]
            for half in range(2):
                mine = core if half else other
                for k in range(chunks):
                    u, i = (p * mine + q * (1 - mine) for p, q in zip(place[slot, k], place[swapped, k]))
                    first = (half * chunks + k) * rows
                    w_buf[u, i, half] = spread[first : first + rows]

    barrier = pltpu.get_barrier_semaphore()
    for dev in (sib, dev_a, dev_b, dev_d):
        pl.semaphore_signal(barrier, inc=1, device_id=dev, device_id_type=MESH)
    for step in range(1, n_z):
        target = (zed + step) % n_z
        pl.semaphore_signal(
            barrier, inc=1, device_id=(seq, target * 2 + core), device_id_type=MESH
        )
    for k in range(chunks):
        load_own(k).start()
    for copy in weight_copies:
        copy.start()
    for k in range(chunks):
        load_own(k).wait()
        norm_own(k)
        if k == 0:
            pl.semaphore_wait(barrier, 4 + n_z - 1)
        if k < 2:
            own_a(k).start()
            own_b(k).start()
        own_sib(k, core).start()
        if k == 0:
            list_own()
            list_copy(A, dev_a).start()
            list_copy(B, dev_b).start()
            list_copy(DIAG, dev_d).start()
    spread_weights()

    def unit(u):
        span = count * 2 * rows
        hidden = columns * inner
        group = hidden // 3
        for n in range(3):
            first = n * group
            x = x_buf[u].reshape(span, width)
            g = dot_nt(x, gate_w[first : first + group])
            up = dot_nt(x, up_w[first : first + group])
            h = silu(g) * up
            for at in range(0, group, LANES):
                i = (first + at) // inner
                weight = w_buf[u, :, :, :, i * LANES : (i + 1) * LANES].reshape(span, LANES)
                hid[:, first + at : first + at + LANES] = (h[:, at : at + LANES] * weight).astype(jnp.bfloat16)
            do(u, n + 1)
        tile = width // 2
        for n in range(2):
            cols = pl.ds(n * tile, tile)
            p = jnp.dot(hid[...], down_w[:, cols], preferred_element_type=jnp.float32)
            part[u, :, :, :, cols] = p.astype(jnp.bfloat16).reshape(count, 2, rows, tile)
            if n == 0:
                do(u, 4)

    def shared_rows(pieces, span):
        take = span.size
        total = len(pieces) * take
        x = jnp.concatenate([x_buf[u, i, core, span] for u, i in pieces], axis=0)
        shid[:total] = (silu(dot_nt(x, sgate_w[...])) * dot_nt(x, sup_w[...])).astype(jnp.bfloat16)
        tile = width // 4

        @pl.loop(0, width // tile)
        def _(n):
            cols = pl.ds(pl.multiple_of(n * tile, tile), tile)
            p = jnp.dot(shid[:total], sdown_w[:, cols], preferred_element_type=jnp.float32)
            for at, (u, i) in enumerate(pieces):
                old = part[u, i, core, span, cols].astype(jnp.float32)
                part[u, i, core, span, cols] = (old + p[at * take : (at + 1) * take]).astype(jnp.bfloat16)

    def among(u, those):
        found = u == those[0]
        for other_unit in those[1:]:
            found = jnp.logical_or(found, u == other_unit)
        return found

    def shared(u):
        if n_z == 4 and chunks == 4:
            every = pl.ds(0, rows)
            owns = [place[OWN, k][0] for k in (0, 2)]
            diags = [place[DIAG, k][0] for k in (0, 2)]
            mixed = [place[A, k][0] for k in (1, 3)]
            is_own = jnp.logical_and(zed == OWN, among(u, owns))
            is_diag = jnp.logical_and(zed == DIAG, among(u, diags))

            @pl.when(jnp.logical_or(is_own, is_diag))
            def _():
                shared_rows([(u, 0), (u, 1)], every)

            @pl.when(jnp.logical_and(jnp.logical_or(zed == A, zed == B), among(u, mixed)))
            def _():
                shared_rows([(u - 1, zed - 1), (u, zed - 1)], every)
        else:
            mine = pl.ds(pl.multiple_of(zed * rows_z, rows_z), rows_z)
            shared_rows([(u, i) for i in range(count)], mine)

    def add_up(at, *terms):
        @pl.loop(0, rows // 32)
        def _(n):
            some = pl.ds(pl.multiple_of(n * 32, 32), 32)
            total = part[(*at, core, some)].astype(jnp.float32)
            for ref, index in terms:
                total = total + ref[(*index, some)].astype(jnp.float32)
            part[(*at, core, some)] = total.astype(jnp.bfloat16)

    def add_pair(k, slot):
        at = place[slot, k]
        part_copy(*at).wait_recv()
        add_up(at, (from_sib, at))

    def step_own(k):
        own_a(k).start()
        own_b(k).start()

    def step_take_b(k):
        net(k, B).wait_recv()
        relay(k).start()
        over_z(k, B).start()
        sib_net(k, B, core).start()

    def step_take_a(k):
        got_net(k, A)

    def step_take_d(k):
        got_net(k, DIAG)

    def step_pass_z(k):
        got_z(k, B)
        got_z(k, A)

    def step_pass_d(k):
        got_z(k, DIAG)

    def step_ring_a(k):
        add_pair(k, A)
        ring_a(k).start()

    def step_pair_b(k):
        add_pair(k, B)

    def step_ring_d(k):
        add_pair(k, DIAG)
        ring_d(k).start()

    def step_pair_own(k):
        add_pair(k, OWN)

    def step_ring_b(k):
        ring_d(k).wait_recv()
        add_up(place[B, k], (ring_in, (k, 0)))
        ring_b(k).start()

    def step_over_z(k):
        ring_a(k).wait_recv()
        ring_b(k).wait_recv()
        add_up(place[OWN, k], (ring_in, (k, 1)), (ring_in, (k, 2)))
        for step in range(1, n_z):
            z_copy(k, zed, (zed + step) % n_z).start()

    actions = {
        "own": step_own,
        "take_b": step_take_b,
        "take_a": step_take_a,
        "take_d": step_take_d,
        "pass_z": step_pass_z,
        "pass_d": step_pass_d,
        "ring_a": step_ring_a,
        "pair_b": step_pair_b,
        "ring_d": step_ring_d,
        "pair_own": step_pair_own,
        "ring_b": step_ring_b,
        "over_z": step_over_z,
    }

    def run(at):
        for name, k in steps.get(at, ()):
            actions[name](k)

    def do(u, point):
        for n in range(len(units)):
            if (n, point) in steps:

                @pl.when(u == n)
                def _():
                    run((n, point))

    def finish(k):
        mine = pl.ds(pl.multiple_of(zed * rows_z, rows_z), rows_z)
        total = part[(*place[OWN, k], core, mine)].astype(jnp.float32)
        for step in range(1, n_z):
            source = (zed + step) % n_z
            z_copy(k, source, source).wait_recv()
            total = total + z_in[k, source].astype(jnp.float32)
        out_ref[k] = total.astype(jnp.bfloat16)

    for copy in weight_copies[:3]:
        copy.wait()

    def ready(n):
        for slot, k in units[n]:
            if slot == OWN:
                own_sib(k, other).wait_recv()
            else:
                got_sib(k, slot)

    @pl.loop(0, len(units))
    def _(u):
        do(u, 0)
        for n in range(len(units)):

            @pl.when(u == n)
            def _():
                ready(n)

        unit(u)
        for i in range(count):
            part_copy(u, i).start()

        @pl.when(u == 0)
        def _():
            for copy in weight_copies[3:]:
                copy.wait()

        shared(u)
        do(u, 5)

    run((len(units), 0))

    for slot, dev in ((A, dev_a), (B, dev_b), (DIAG, dev_d)):
        list_copy(slot, dev).wait_send()

    for k in range(chunks):
        finish(k)
    for k in range(chunks):
        own_sib(k, core).wait_send()
        own_a(k).wait_send()
        own_b(k).wait_send()
        relay(k).wait_send()
        for slot in (A, B, DIAG):
            over_z(k, slot).wait_send()
            sib_net(k, slot, core).wait_send()
            sib_z(k, slot, core).wait_send()
        ring_d(k).wait_send()
        ring_a(k).wait_send()
        ring_b(k).wait_send()
        for step in range(1, n_z):
            z_copy(k, zed, (zed + step) % n_z).wait_send()
    for u in range(len(units)):
        for i in range(count):
            part_copy(u, i).wait_send()


def on_device(
    tokens,
    expert_ids,
    gate_weights,
    live,
    norm_gain,
    expert_gate,
    expert_up,
    expert_down,
    shared_gate,
    shared_up,
    shared_down,
):
    tok_seq, width = tokens.shape
    columns, inner = expert_gate.shape[:2]
    s_inner = shared_gate.shape[0]
    n_seq = lax.axis_size("seq")
    n_tp = lax.axis_size("tp")
    assert n_seq == 4
    tok_dev = tok_seq // n_tp
    n_z = n_tp // 2
    chunks = 4 if tok_dev >= 64 else 1
    rows_z = tok_dev // chunks
    rows = n_z * rows_z
    assert rows_z & (rows_z - 1) == 0 and chunks & (chunks - 1) == 0
    experts = columns * n_tp
    listed = -(-experts // 16) * 16
    n_units, count = (len(UNITS), 2) if chunks == 4 else (len(UNITS_ONE), 1)

    bf16 = jnp.bfloat16
    dma = pltpu.SemaphoreType.DMA
    vmem = pl.BlockSpec(memory_space=pltpu.VMEM)
    out = pl.pallas_call(
        partial(layer_kernel, chunks, n_z, columns, width, rows_z),
        out_shape=jax.ShapeDtypeStruct((chunks, rows_z, width), bf16),
        in_specs=[pl.BlockSpec(memory_space=pl.ANY), vmem, vmem, vmem, vmem]
        + [pl.BlockSpec(memory_space=pl.ANY)] * 6,
        out_specs=vmem,
        scratch_shapes=[
            pltpu.VMEM((n_units, count, 2, rows, width), bf16),
            pltpu.VMEM((n_units, count, 2, rows, width), bf16),
            pltpu.VMEM((n_units, count, rows, width), bf16),
            pltpu.VMEM((chunks, 3, rows, width), bf16),
            pltpu.VMEM((chunks, n_z, rows_z, width), bf16),
            pltpu.VMEM((columns * inner, width), bf16),
            pltpu.VMEM((columns * inner, width), bf16),
            pltpu.VMEM((columns * inner, width), bf16),
            pltpu.VMEM((s_inner, width), bf16),
            pltpu.VMEM((s_inner, width), bf16),
            pltpu.VMEM((s_inner, width), bf16),
            pltpu.VMEM((count * 2 * rows, columns * inner), bf16),
            pltpu.VMEM((2 * rows, s_inner), bf16),
            pltpu.VMEM((chunks, n_z, rows_z, width), bf16),
            pltpu.VMEM((4, listed, tok_seq), bf16),
            pltpu.VMEM((n_units, count, 2, rows, columns * LANES), jnp.float32),
            dma((6,)),
            dma((chunks,)),
            dma((3,)),
            dma((chunks, 3)),
            dma((chunks, 10)),
            dma((n_units, count)),
            dma((chunks, 3)),
            dma((chunks, n_z)),
            dma((3,)),
            dma((chunks, 4, 4)),
            dma((n_units, count)),
            dma((chunks, 3)),
            dma((chunks, n_z)),
        ],
        compiler_params=pltpu.CompilerParams(
            collective_id=0, has_side_effects=True, vmem_limit_bytes=62 * 1024 * 1024
        ),
    )(
        tokens.reshape(n_z, 2, chunks, rows_z, width),
        norm_gain,
        expert_ids.T,
        gate_weights.T,
        live,
        expert_gate.reshape(columns * inner, width),
        expert_up.reshape(columns * inner, width),
        expert_down.reshape(columns * inner, width),
        shared_gate,
        shared_up,
        shared_down,
    )
    return out.reshape(tok_dev, width)


def solution(mesh):
    placed = (
        P("seq", None),
        P("seq", None),
        P("seq", None),
        P("seq"),
        P(),
        P("tp", "seq", None),
        P("tp", "seq", None),
        P("tp", "seq", None),
        P("seq", None),
        P("seq", None),
        P("seq", None),
    )
    return jax.shard_map(
        on_device, mesh=mesh, in_specs=placed, out_specs=P(("seq", "tp"), None), check_vma=False
    )
```

```python
import math
from functools import partial

import jax
import jax.numpy as jnp
from jax import lax
from jax.experimental import pallas as pl
from jax.experimental.pallas import tpu as pltpu
from jax.sharding import PartitionSpec as P

MESH = pl.DeviceIdType.MESH
LANES = 128
OWN, A, B, DIAG = 0, 1, 2, 3
UNITS = (
    ((OWN, 0), (OWN, 1)),
    ((OWN, 2), (OWN, 3)),
    ((A, 0), (B, 0)),
    ((A, 1), (B, 1)),
    ((DIAG, 0), (DIAG, 1)),
    ((A, 2), (B, 2)),
    ((A, 3), (B, 3)),
    ((DIAG, 2), (DIAG, 3)),
)
UNITS_ONE = (((OWN, 0),), ((A, 0),), ((B, 0),), ((DIAG, 0),))
STEPS = {
    (0, 0): (("take_a", 0),),
    (0, 1): (("take_b", 0),),
    (1, 1): (("take_b", 1),),
    (1, 2): (("own", 2),),
    (1, 3): (("take_a", 1), ("pair_own", 1), ("pass_z", 0),),
    (2, 0): (("take_d", 0), ("own", 3),),
    (2, 1): (("take_d", 1),),
    (2, 2): (("pair_own", 3), ("pair_own", 0),),
    (2, 3): (("take_b", 2), ("pass_z", 1),),
    (3, 1): (("take_a", 2),),
    (3, 2): (("take_b", 3),),
    (3, 3): (("pass_d", 0),),
    (4, 0): (("pass_d", 1), ("ring_a", 1), ("ring_a", 0), ("take_a", 3),),
    (4, 2): (("pair_own", 2),),
    (4, 3): (("pass_z", 2),),
    (4, 5): (("take_d", 3),),
    (5, 1): (("take_d", 2),),
    (5, 2): (("pair_b", 1), ("ring_d", 1),),
    (5, 3): (("ring_d", 0), ("pass_z", 3),),
    (6, 3): (("ring_b", 1), ("pair_b", 0), ("pair_b", 2), ("pass_d", 3),),
    (6, 5): (("ring_a", 2),),
    (7, 0): (("pass_d", 2), ("ring_b", 0),),
    (7, 5): (("over_z", 1), ("pair_b", 3),),
    (8, 0): (("ring_d", 2), ("over_z", 0), ("ring_d", 3), ("ring_b", 2), ("ring_b", 3), ("ring_a", 3), ("over_z", 2), ("over_z", 3),),
}
SHARES = ((8, 8), (8, 8), (8, 8), (8, 8))
SHARES_ONE = ((5, 5),)
STEPS_ONE = {
    (0, 5): (("take_b", 0), ("take_a", 0), ("pass_z", 0)),
    (1, 5): (("take_d", 0),),
    (2, 5): (("pass_d", 0), ("ring_a", 0), ("pair_b", 0)),
    (4, 0): (("ring_d", 0), ("pair_own", 0), ("ring_b", 0), ("over_z", 0)),
}


def dot_nt(a, b):
    return lax.dot_general(a, b, (((1,), (1,)), ((), ())), preferred_element_type=jnp.float32)


def silu(v):
    return v / (1.0 + jnp.exp(-v))


def layer_kernel(
    chunks,
    n_z,
    columns,
    width,
    rows_z,
    tok_hbm,
    gain_ref,
    ids_ref,
    gates_ref,
    live_ref,
    gate_hbm,
    up_hbm,
    down_hbm,
    sgate_hbm,
    sup_hbm,
    sdown_hbm,
    out_ref,
    x_buf,
    part,
    from_sib,
    ring_in,
    z_in,
    gate_w,
    up_w,
    down_w,
    sgate_w,
    sup_w,
    sdown_w,
    hid,
    shid,
    tok_v,
    lists,
    w_buf,
    w_sem,
    own_sem,
    send_list,
    send_own,
    send_fwd,
    send_part,
    send_ring,
    send_z,
    recv_list,
    recv_x,
    recv_part,
    recv_ring,
    recv_z,
):
    seq = lax.axis_index("seq")
    tp = lax.axis_index("tp")
    core = tp % 2
    zed = tp // 2
    other = 1 - core
    sx = seq % 2
    sy = seq // 2
    nbr_x = sy * 2 + (1 - sx)
    nbr_y = (1 - sy) * 2 + sx
    sib = (seq, zed * 2 + other)
    dev_a = (nbr_y * other + nbr_x * core, tp)
    dev_b = (nbr_x * other + nbr_y * core, tp)
    dev_d = (3 - seq, tp)
    rows = n_z * rows_z
    parity = zed % 2
    dev_z = (seq, (zed + 1 - 2 * parity) * 2 + core)
    def share_of(k, slot):
        return width * shares[k][slot == DIAG] // 20 // LANES * LANES

    def fetched(k, slot):
        share = share_of(k, slot)
        return pl.ds(pl.multiple_of(parity * share, LANES), width - share)

    def passed(k, slot):
        share = share_of(k, slot)
        return pl.ds(pl.multiple_of(parity * (width - share), LANES), share)

    def given(k, slot):
        share = share_of(k, slot)
        return pl.ds(pl.multiple_of((1 - parity) * (width - share), LANES), share)

    whole = pl.ds(0, width)
    inner = gate_w.shape[0] // columns
    tok_seq = ids_ref.shape[1]
    units, steps, shares = (UNITS, STEPS, SHARES) if chunks == 4 else (UNITS_ONE, STEPS_ONE, SHARES_ONE)
    place = {which: (u, i) for u, unit in enumerate(units) for i, which in enumerate(unit)}
    count = len(units[0])

    def remote(src, dst, ssem, rsem, dev):
        return pltpu.make_async_remote_copy(
            src_ref=src, dst_ref=dst, send_sem=ssem, recv_sem=rsem, device_id=dev, device_id_type=MESH
        )

    def x_copy(k, src_slot, dst_slot, half, cols, ssem, kind, dev):
        return remote(
            x_buf.at[(*place[src_slot, k], half, slice(None), cols)],
            x_buf.at[(*place[dst_slot, k], half, slice(None), cols)],
            ssem,
            recv_x.at[k, dst_slot, kind],
            dev,
        )

    def own_a(k):
        return x_copy(k, OWN, A, core, fetched(k, A), send_own.at[k, 1], 0, dev_a)

    def own_b(k):
        return x_copy(k, OWN, B, core, fetched(k, B), send_own.at[k, 2], 0, dev_b)

    def own_sib(k, half):
        return x_copy(k, OWN, OWN, half, whole, send_own.at[k, 0], 2, sib)

    def net(k, slot):
        return x_copy(k, slot, slot, core, fetched(k, slot), send_fwd.at[k, 0], 0, dev_a)

    def relay(k):
        return x_copy(k, B, DIAG, core, fetched(k, DIAG), send_fwd.at[k, 0], 0, dev_a)

    def over_z(k, slot):
        return x_copy(k, slot, slot, core, passed(k, slot), send_fwd.at[k, slot], 1, dev_z)

    def from_z(k, slot):
        return x_copy(k, slot, slot, core, given(k, slot), send_fwd.at[k, slot], 1, dev_z)

    def sib_net(k, slot, half):
        return x_copy(k, slot, slot, half, fetched(k, slot), send_fwd.at[k, slot + 3], 2, sib)

    def sib_z(k, slot, half):
        return x_copy(k, slot, slot, half, given(k, slot), send_fwd.at[k, slot + 6], 3, sib)

    def got_net(k, slot):
        net(k, slot).wait_recv()
        over_z(k, slot).start()
        sib_net(k, slot, core).start()

    def got_z(k, slot):
        from_z(k, slot).wait_recv()
        sib_z(k, slot, core).start()

    def got_sib(k, slot):
        sib_net(k, slot, other).wait_recv()
        sib_z(k, slot, other).wait_recv()

    def list_copy(slot, dev):
        return remote(lists.at[OWN], lists.at[slot], send_list.at[slot - 1], recv_list.at[slot - 1], dev)

    def part_copy(u, i):
        return remote(part.at[u, i, other], from_sib.at[u, i], send_part.at[u, i], recv_part.at[u, i], sib)

    def ring_copy(k, slot, leg, dev):
        return remote(
            part.at[(*place[slot, k], core)],
            ring_in.at[k, leg],
            send_ring.at[k, leg],
            recv_ring.at[k, leg],
            dev,
        )

    def ring_d(k):
        return ring_copy(k, DIAG, 0, dev_a)

    def ring_a(k):
        return ring_copy(k, A, 1, dev_a)

    def ring_b(k):
        return ring_copy(k, B, 2, dev_b)

    def z_copy(k, src_z, dst_z):
        return remote(
            part.at[(*place[OWN, k], core, pl.ds(dst_z * rows_z, rows_z))],
            z_in.at[k, src_z],
            send_z.at[k, dst_z],
            recv_z.at[k, src_z],
            (seq, dst_z * 2 + core),
        )

    weight_copies = [
        pltpu.make_async_copy(src, dst, w_sem.at[i])
        for i, (src, dst) in enumerate(
            (
                (gate_hbm, gate_w),
                (up_hbm, up_w),
                (down_hbm, down_w),
                (sgate_hbm, sgate_w),
                (sup_hbm, sup_w),
                (sdown_hbm, sdown_w),
            )
        )
    ]

    def load_own(k):
        return pltpu.make_async_copy(tok_hbm.at[:, core, k], tok_v.at[k], own_sem.at[k])

    def norm_own(k):
        values = tok_v[k].reshape(rows, width).astype(jnp.float32)
        scale = lax.rsqrt(jnp.mean(values * values, axis=-1, keepdims=True) + 1e-05)
        gain = gain_ref[...].reshape(1, width)
        x_buf[(*place[OWN, k], core)] = (values * scale * gain).astype(jnp.bfloat16)

    def list_own():
        weight = gates_ref[...].astype(jnp.float32) * live_ref[...].reshape(1, tok_seq).astype(jnp.float32)
        expert = lax.broadcasted_iota(jnp.int32, lists.shape[1:], 0)
        total = jnp.zeros(lists.shape[1:], jnp.float32)
        for j in range(ids_ref.shape[0]):
            total = total + jnp.where(ids_ref[j : j + 1] == expert, weight[j : j + 1], 0.0)
        lists[OWN] = total.astype(jnp.bfloat16)

    def spread_weights():
        token = lax.broadcasted_iota(jnp.int32, (1, tok_seq), 1)
        bits_r = rows_z.bit_length() - 1
        bits_k = chunks.bit_length() - 1
        at_r = token & (rows_z - 1)
        at_k = (token >> bits_r) & (chunks - 1)
        at_half = (token >> (bits_r + bits_k)) & 1
        at_z = token >> (bits_r + bits_k + 1)
        spot = (at_half * chunks + at_k) * rows + at_z * rows_z + at_r
        row = lax.broadcasted_iota(jnp.int32, (tok_seq, tok_seq), 0)
        onehot = jnp.where(row == spot, 1.0, 0.0).astype(jnp.bfloat16)
        expert = lax.broadcasted_iota(jnp.int32, lists.shape[1:], 0)
        for slot in range(4):
            if slot:
                list_copy(slot, dev_a).wait_recv()
            listed = lists[slot].astype(jnp.float32)
            picked = []
            for i in range(columns):
                mine = jnp.where(expert == tp * columns + i, listed, 0.0)
                mine = jnp.sum(mine, axis=0, keepdims=True)
                picked.append(jnp.broadcast_to(mine, (LANES, tok_seq)))
            spread = dot_nt(onehot, jnp.concatenate(picked, axis=0).astype(jnp.bfloat16))
            swapped = {OWN: OWN, A: B, B: A, DIAG: DIAG}[slot]
            for half in range(2):
                mine = core if half else other
                for k in range(chunks):
                    u, i = (p * mine + q * (1 - mine) for p, q in zip(place[slot, k], place[swapped, k]))
                    first = (half * chunks + k) * rows
                    w_buf[u, i, half] = spread[first : first + rows]

    barrier = pltpu.get_barrier_semaphore()
    for dev in (sib, dev_a, dev_b, dev_d):
        pl.semaphore_signal(barrier, inc=1, device_id=dev, device_id_type=MESH)
    for step in range(1, n_z):
        target = (zed + step) % n_z
        pl.semaphore_signal(
            barrier, inc=1, device_id=(seq, target * 2 + core), device_id_type=MESH
        )
    for k in range(chunks):
        load_own(k).start()
    for copy in weight_copies:
        copy.start()
    for k in range(chunks):
        load_own(k).wait()
        norm_own(k)
        if k == 0:
            pl.semaphore_wait(barrier, 4 + n_z - 1)
        if k < 2:
            own_a(k).start()
            own_b(k).start()
        own_sib(k, core).start()
        if k == 0:
            list_own()
            list_copy(A, dev_a).start()
            list_copy(B, dev_b).start()
            list_copy(DIAG, dev_d).start()
    spread_weights()

    def unit(u):
        span = count * 2 * rows
        hidden = columns * inner
        group = hidden // 3
        for n in range(3):
            first = n * group
            x = x_buf[u].reshape(span, width)
            g = dot_nt(x, gate_w[first : first + group])
            up = dot_nt(x, up_w[first : first + group])
            h = silu(g) * up
            for at in range(0, group, LANES):
                i = (first + at) // inner
                weight = w_buf[u, :, :, :, i * LANES : (i + 1) * LANES].reshape(span, LANES)
                hid[:, first + at : first + at + LANES] = (h[:, at : at + LANES] * weight).astype(jnp.bfloat16)
            do(u, n + 1)

        @pl.when(u == 0)
        def _():
            weight_copies[2].wait()

        tile = width // 2
        for n in range(2):
            cols = pl.ds(n * tile, tile)
            p = jnp.dot(hid[...], down_w[:, cols], preferred_element_type=jnp.float32)
            part[u, :, :, :, cols] = p.astype(jnp.bfloat16).reshape(count, 2, rows, tile)
            if n == 0:
                do(u, 4)

    def shared_rows(pieces, span):
        take = span.size
        total = len(pieces) * take
        x = jnp.concatenate([x_buf[u, i, core, span] for u, i in pieces], axis=0)
        shid[:total] = (silu(dot_nt(x, sgate_w[...])) * dot_nt(x, sup_w[...])).astype(jnp.bfloat16)
        tile = width // 4

        @pl.loop(0, width // tile)
        def _(n):
            cols = pl.ds(pl.multiple_of(n * tile, tile), tile)
            p = jnp.dot(shid[:total], sdown_w[:, cols], preferred_element_type=jnp.float32)
            for at, (u, i) in enumerate(pieces):
                old = part[u, i, core, span, cols].astype(jnp.float32)
                part[u, i, core, span, cols] = (old + p[at * take : (at + 1) * take]).astype(jnp.bfloat16)

    def among(u, those):
        found = u == those[0]
        for other_unit in those[1:]:
            found = jnp.logical_or(found, u == other_unit)
        return found

    def shared(u):
        if n_z == 4 and chunks == 4:
            every = pl.ds(0, rows)
            owns = [place[OWN, k][0] for k in (0, 2)]
            diags = [place[DIAG, k][0] for k in (0, 2)]
            mixed = [place[A, k][0] for k in (1, 3)]
            is_own = jnp.logical_and(zed == OWN, among(u, owns))
            is_diag = jnp.logical_and(zed == DIAG, among(u, diags))

            @pl.when(jnp.logical_or(is_own, is_diag))
            def _():
                shared_rows([(u, 0), (u, 1)], every)

            @pl.when(jnp.logical_and(jnp.logical_or(zed == A, zed == B), among(u, mixed)))
            def _():
                shared_rows([(u - 1, zed - 1), (u, zed - 1)], every)
        else:
            mine = pl.ds(pl.multiple_of(zed * rows_z, rows_z), rows_z)
            shared_rows([(u, i) for i in range(count)], mine)

    def add_up(at, *terms):
        @pl.loop(0, rows // 32)
        def _(n):
            some = pl.ds(pl.multiple_of(n * 32, 32), 32)
            total = part[(*at, core, some)].astype(jnp.float32)
            for ref, index in terms:
                total = total + ref[(*index, some)].astype(jnp.float32)
            part[(*at, core, some)] = total.astype(jnp.bfloat16)

    def add_pair(k, slot):
        at = place[slot, k]
        part_copy(*at).wait_recv()
        add_up(at, (from_sib, at))

    def step_own(k):
        own_a(k).start()
        own_b(k).start()

    def step_take_b(k):
        net(k, B).wait_recv()
        relay(k).start()
        over_z(k, B).start()
        sib_net(k, B, core).start()

    def step_take_a(k):
        got_net(k, A)

    def step_take_d(k):
        got_net(k, DIAG)

    def step_pass_z(k):
        got_z(k, B)
        got_z(k, A)

    def step_pass_d(k):
        got_z(k, DIAG)

    def step_ring_a(k):
        add_pair(k, A)
        ring_a(k).start()

    def step_pair_b(k):
        add_pair(k, B)

    def step_ring_d(k):
        add_pair(k, DIAG)
        ring_d(k).start()

    def step_pair_own(k):
        add_pair(k, OWN)

    def step_ring_b(k):
        ring_d(k).wait_recv()
        add_up(place[B, k], (ring_in, (k, 0)))
        ring_b(k).start()

    def step_over_z(k):
        ring_a(k).wait_recv()
        ring_b(k).wait_recv()
        add_up(place[OWN, k], (ring_in, (k, 1)), (ring_in, (k, 2)))
        for step in range(1, n_z):
            z_copy(k, zed, (zed + step) % n_z).start()

    actions = {
        "own": step_own,
        "take_b": step_take_b,
        "take_a": step_take_a,
        "take_d": step_take_d,
        "pass_z": step_pass_z,
        "pass_d": step_pass_d,
        "ring_a": step_ring_a,
        "pair_b": step_pair_b,
        "ring_d": step_ring_d,
        "pair_own": step_pair_own,
        "ring_b": step_ring_b,
        "over_z": step_over_z,
    }

    def run(at):
        for name, k in steps.get(at, ()):
            actions[name](k)

    def do(u, point):
        for n in range(len(units)):
            if (n, point) in steps:

                @pl.when(u == n)
                def _():
                    run((n, point))

    def finish(k):
        mine = pl.ds(pl.multiple_of(zed * rows_z, rows_z), rows_z)
        total = part[(*place[OWN, k], core, mine)].astype(jnp.float32)
        for step in range(1, n_z):
            source = (zed + step) % n_z
            z_copy(k, source, source).wait_recv()
            total = total + z_in[k, source].astype(jnp.float32)
        out_ref[k] = total.astype(jnp.bfloat16)

    for copy in weight_copies[:2]:
        copy.wait()

    def ready(n):
        for slot, k in units[n]:
            if slot == OWN:
                own_sib(k, other).wait_recv()
            else:
                got_sib(k, slot)

    @pl.loop(0, len(units))
    def _(u):
        do(u, 0)
        for n in range(len(units)):

            @pl.when(u == n)
            def _():
                ready(n)

        unit(u)
        for i in range(count):
            part_copy(u, i).start()

        @pl.when(u == 0)
        def _():
            for copy in weight_copies[3:]:
                copy.wait()

        shared(u)
        do(u, 5)

    run((len(units), 0))

    for slot, dev in ((A, dev_a), (B, dev_b), (DIAG, dev_d)):
        list_copy(slot, dev).wait_send()

    for k in range(chunks):
        finish(k)
    for k in range(chunks):
        own_sib(k, core).wait_send()
        own_a(k).wait_send()
        own_b(k).wait_send()
        relay(k).wait_send()
        for slot in (A, B, DIAG):
            over_z(k, slot).wait_send()
            sib_net(k, slot, core).wait_send()
            sib_z(k, slot, core).wait_send()
        ring_d(k).wait_send()
        ring_a(k).wait_send()
        ring_b(k).wait_send()
        for step in range(1, n_z):
            z_copy(k, zed, (zed + step) % n_z).wait_send()
    for u in range(len(units)):
        for i in range(count):
            part_copy(u, i).wait_send()


def on_device(
    tokens,
    expert_ids,
    gate_weights,
    live,
    norm_gain,
    expert_gate,
    expert_up,
    expert_down,
    shared_gate,
    shared_up,
    shared_down,
):
    tok_seq, width = tokens.shape
    columns, inner = expert_gate.shape[:2]
    s_inner = shared_gate.shape[0]
    n_seq = lax.axis_size("seq")
    n_tp = lax.axis_size("tp")
    assert n_seq == 4
    tok_dev = tok_seq // n_tp
    n_z = n_tp // 2
    chunks = 4 if tok_dev >= 64 else 1
    rows_z = tok_dev // chunks
    rows = n_z * rows_z
    assert rows_z & (rows_z - 1) == 0 and chunks & (chunks - 1) == 0
    experts = columns * n_tp
    listed = -(-experts // 16) * 16
    n_units, count = (len(UNITS), 2) if chunks == 4 else (len(UNITS_ONE), 1)

    bf16 = jnp.bfloat16
    dma = pltpu.SemaphoreType.DMA
    vmem = pl.BlockSpec(memory_space=pltpu.VMEM)
    out = pl.pallas_call(
        partial(layer_kernel, chunks, n_z, columns, width, rows_z),
        out_shape=jax.ShapeDtypeStruct((chunks, rows_z, width), bf16),
        in_specs=[pl.BlockSpec(memory_space=pl.ANY), vmem, vmem, vmem, vmem]
        + [pl.BlockSpec(memory_space=pl.ANY)] * 6,
        out_specs=vmem,
        scratch_shapes=[
            pltpu.VMEM((n_units, count, 2, rows, width), bf16),
            pltpu.VMEM((n_units, count, 2, rows, width), bf16),
            pltpu.VMEM((n_units, count, rows, width), bf16),
            pltpu.VMEM((chunks, 3, rows, width), bf16),
            pltpu.VMEM((chunks, n_z, rows_z, width), bf16),
            pltpu.VMEM((columns * inner, width), bf16),
            pltpu.VMEM((columns * inner, width), bf16),
            pltpu.VMEM((columns * inner, width), bf16),
            pltpu.VMEM((s_inner, width), bf16),
            pltpu.VMEM((s_inner, width), bf16),
            pltpu.VMEM((s_inner, width), bf16),
            pltpu.VMEM((count * 2 * rows, columns * inner), bf16),
            pltpu.VMEM((2 * rows, s_inner), bf16),
            pltpu.VMEM((chunks, n_z, rows_z, width), bf16),
            pltpu.VMEM((4, listed, tok_seq), bf16),
            pltpu.VMEM((n_units, count, 2, rows, columns * LANES), jnp.float32),
            dma((6,)),
            dma((chunks,)),
            dma((3,)),
            dma((chunks, 3)),
            dma((chunks, 10)),
            dma((n_units, count)),
            dma((chunks, 3)),
            dma((chunks, n_z)),
            dma((3,)),
            dma((chunks, 4, 4)),
            dma((n_units, count)),
            dma((chunks, 3)),
            dma((chunks, n_z)),
        ],
        compiler_params=pltpu.CompilerParams(
            collective_id=0, has_side_effects=True, vmem_limit_bytes=62 * 1024 * 1024
        ),
    )(
        tokens.reshape(n_z, 2, chunks, rows_z, width),
        norm_gain,
        expert_ids.T,
        gate_weights.T,
        live,
        expert_gate.reshape(columns * inner, width),
        expert_up.reshape(columns * inner, width),
        expert_down.reshape(columns * inner, width),
        shared_gate,
        shared_up,
        shared_down,
    )
    return out.reshape(tok_dev, width)


def solution(mesh):
    placed = (
        P("seq", None),
        P("seq", None),
        P("seq", None),
        P("seq"),
        P(),
        P("tp", "seq", None),
        P("tp", "seq", None),
        P("tp", "seq", None),
        P("seq", None),
        P("seq", None),
        P("seq", None),
    )
    return jax.shard_map(
        on_device, mesh=mesh, in_specs=placed, out_specs=P(("seq", "tp"), None), check_vma=False
    )
```
